128 devices in a mesh: blk: 2 (over core), smp: 64 (over z, y, x).
Axes of the slice: x: 4, y: 4, z: 4, core: 2. Of those that a mesh axis runs over, the one named last changes fastest.
Arguments:
- genotypes: bfloat16 [2, 65536, 2048], P('blk', 'smp'), may hold values from -2 to 10, as said below
- sizes: int32 [2], P('blk'), may hold values from 1024 to 2048, as said below
- start: float32 [2, 2048, 256], P('blk', 'smp'), may hold values from -6 to 6
Outputs:
- basis: float32 [2, 2048, 256], P('blk', 'smp')
- scaled: float32 [2, 256, 256], P('blk')
The draws below stay inside these ranges and needn't reach their ends.
Inputs may be any that keep to these rules, and one draw needn't show every extreme that they name: `sizes`: at least one block has exactly 2048 SNPs. `genotypes`: each column is a standardized count of 0, 1 or 2 alleles; columns at or past a block's size hold values that the block does not use.
All inputs are finite; a program needn't handle non-finite values.
Results may differ from the reference program's by a relative error of at most 0.0003.
Values may be sent and summed in bfloat16 or wider, within the bound.
A program may use at most 128 MiB of HBM per device.

```python
import jax
import jax.numpy as jnp
from jax import lax

CAP = 2048
K = 256
ITERS = 2
SAMPLES = 65536
NBLK = 2


def haplotype(key, freqs):
    first, second = jax.random.split(key)
    latent = jax.random.uniform(first, (NBLK, SAMPLES, CAP), jnp.float32)
    fresh = jax.random.randint(second, (NBLK, SAMPLES, CAP), 0, 10, jnp.int32) == 0
    places = lax.broadcasted_iota(jnp.int32, (NBLK, SAMPLES, CAP), 2)
    breaks = jnp.logical_or(fresh, places == 0)
    anchor = lax.cummax(jnp.where(breaks, places, jnp.int32(0)), axis=2)
    copied = jnp.take_along_axis(latent, anchor, axis=2)
    return (copied < freqs).astype(jnp.float32)


def draw_genotypes(key, part):
    first, second, third = jax.random.split(jax.random.fold_in(key, 11), 3)
    freqs = jax.random.uniform(first, (NBLK, 1, CAP), jnp.float32, 0.05, 0.5)
    dosage = haplotype(second, freqs) + haplotype(third, freqs)
    scaled = (dosage - 2.0 * freqs) / jnp.sqrt(2.0 * freqs * (1.0 - freqs))
    return scaled.astype(jnp.bfloat16)


def draw_sizes(key, part):
    first, second = jax.random.split(jax.random.fold_in(key, 7))
    counts = jax.random.randint(first, (NBLK,), CAP // 2, CAP, jnp.int32)
    chosen = jax.random.randint(second, (), 0, NBLK, jnp.int32)
    places = jnp.arange(NBLK, dtype=jnp.int32)
    return jnp.where(places == chosen, jnp.int32(CAP), counts).astype(jnp.int32)


def block_scale(own_key, dims, shards, least, largest):
    gain, own = 1.0, jax.random.fold_in(own_key, 6)
    for dim, shards_of in shards:
        draws = jnp.exp(jax.random.uniform(jax.random.fold_in(own, dim), (shards_of,), jnp.float32, least / len(shards), largest / len(shards)))
        gain = gain * jnp.repeat(draws, dims[dim] // shards_of).reshape([-1 if axis == dim else 1 for axis in range(len(dims))])
    return gain


def noise(rng, shape, spread, limit, shards=(), kind=jnp.bfloat16):
    array = jax.random.normal(rng, shape, jnp.float32) * spread
    if len(shards) > 0:
        array = block_scale(rng, shape, shards, -0.22, 0.18) * array
    return jnp.clip(array, min=-limit, max=limit).astype(kind)


def setup_inputs(seed: int = 0) -> dict:
    key_list = jax.random.split(jax.random.key(seed), 4)
    return {
        "genotypes": draw_genotypes(jax.random.fold_in(key_list[3], 71), 0),
        "sizes": draw_sizes(jax.random.fold_in(key_list[3], 71), 0),
        "start": noise(key_list[2], (NBLK, CAP, K), 1.0, 6.0, ((0, 2), (1, 64)), jnp.float32),
    }


def one_block(operands):
    dosages, count, vectors = operands
    live = (jnp.arange(CAP, dtype=jnp.int32) < count).astype(jnp.bfloat16)
    masked = dosages * live[None, :]
    gram = jnp.dot(masked.T.astype(jnp.float32), masked.astype(jnp.float32), preferred_element_type=jnp.float32) / SAMPLES
    for repeat in range(ITERS):
        image = jnp.dot(gram.astype(jnp.float32), vectors.astype(jnp.float32), precision=lax.Precision.HIGHEST, preferred_element_type=jnp.float32)
        inner = jnp.dot(image.T.astype(jnp.float32), image.astype(jnp.float32), precision=lax.Precision.HIGHEST, preferred_element_type=jnp.float32)
        lower = jnp.linalg.cholesky(inner)
        vectors = lax.linalg.triangular_solve(lower, image, left_side=False, lower=True, transpose_a=True)
    image = jnp.dot(gram.astype(jnp.float32), vectors.astype(jnp.float32), precision=lax.Precision.HIGHEST, preferred_element_type=jnp.float32)
    rayleigh = jnp.dot(vectors.T.astype(jnp.float32), image.astype(jnp.float32), precision=lax.Precision.HIGHEST, preferred_element_type=jnp.float32)
    return (vectors, rayleigh)

def reference(genotypes, sizes, start):
    vectors, rayleigh = lax.map(one_block, (genotypes, sizes, start))
    total = jnp.sum(jnp.trace(rayleigh, axis1=1, axis2=2))
    scaled = rayleigh * (NBLK * K) / total
    basis = vectors * jnp.sqrt(jnp.float32(CAP))
    return (basis, scaled)
```

```python
import functools
import math

import jax
import jax.numpy as jnp
from jax import lax
from jax.experimental import pallas as pl
from jax.experimental.pallas import tpu as pltpu
from jax.sharding import PartitionSpec as P

CAP = 2048
K = 256
F32 = jnp.float32
BF16 = jnp.bfloat16
MESH = pl.DeviceIdType.MESH
ORDERS = ((0, 1, 2), (1, 2, 0), (2, 0, 1))
SUM_ROWS = ((0, 24), (24, 24), (48, 16))
GATHER_ROWS = ((0, 48), (48, 48), (96, 32))


def split3(v):
    high = v.astype(BF16).astype(F32)
    rest = v - high
    middle = rest.astype(BF16).astype(F32)
    return high, middle, rest - middle


def exact(a, b, dims):
    return lax.dot_general(
        a, b, (dims, ((), ())), precision=lax.Precision.HIGHEST, preferred_element_type=F32
    )


def factor8(block):
    sub = lax.broadcasted_iota(jnp.int32, (8, 128), 0)
    a = {}
    for s in range(8):
        column = jnp.broadcast_to(block[:, s : s + 1], (8, 128))
        for t in range(s, 8):
            a[t, s] = jnp.broadcast_to(column[t : t + 1, :], (8, 128))
    inv = []
    for s in range(8):
        r = lax.rsqrt(a[s, s])
        inv.append(r)
        for t in range(s + 1, 8):
            a[t, s] = a[t, s] * r
        for t in range(s + 1, 8):
            for u in range(s + 1, t + 1):
                a[t, u] = a[t, u] - a[t, s] * a[u, s]
    w = {}
    for s in range(8):
        w[s, s] = inv[s]
        for t in range(s + 1, 8):
            acc = a[t, s] * w[s, s]
            for u in range(s + 1, t):
                acc = acc + a[t, u] * w[u, s]
            w[t, s] = -acc * inv[t]
    columns = []
    for s in range(8):
        col = jnp.where(sub == s, w[s, s], 0.0)
        for t in range(s + 1, 8):
            col = jnp.where(sub == t, w[t, s], col)
        columns.append(col)
    return columns


def factor_group(aug, half, g):
    first = half * 128
    row = pl.multiple_of(first + g * 8, 8)
    panel = aug[pl.ds(row, 8), :]
    block = pltpu.roll(panel[:, first : first + 128], lax.rem(128 - g * 8, 128), 1)
    columns = factor8(block)
    u = None
    for s in range(8):
        term = jnp.concatenate([columns[s]] * 4, axis=1) * jnp.broadcast_to(panel[s : s + 1, :], (8, 512))
        u = term if u is None else u + term
    aug[pl.ds(row, 8), :] = u
    left = u[:, first:256]
    lane = lax.broadcasted_iota(jnp.int32, left.shape, 1) + first
    left = jnp.where(lane > row + 7, left, 0.0)
    lh, lm, ll = split3(left)
    uh, um, ul = split3(u)
    lhs = jnp.concatenate([lh, lh, lm, lm, lh, ll], axis=0).astype(BF16)
    rhs = jnp.concatenate([uh, um, uh, um, ul, uh], axis=0).astype(BF16)
    update = lax.dot_general(lhs, rhs, (((0,), (0,)), ((), ())), preferred_element_type=F32)
    aug[first:256, :] = aug[first:256, :] - update


def factor_start(aug, inner):
    aug[:, 0:256] = inner
    r = lax.broadcasted_iota(jnp.int32, (256, 256), 0)
    c = lax.broadcasted_iota(jnp.int32, (256, 256), 1)
    aug[:, 256:512] = jnp.where(r == c, 1.0, 0.0).astype(F32)


def factor_quarter(aug, quarter):
    @pl.loop(8 * (quarter % 2), 8 * (quarter % 2) + 8)
    def _(g):
        factor_group(aug, quarter // 2, g)


def symmetric(high, low):
    tall = (((0,), (0,)), ((), ()))
    first = lax.dot_general(high, jnp.concatenate([high, low], axis=1), tall, preferred_element_type=F32)
    last = lax.dot_general(low, low, tall, preferred_element_type=F32)
    return first, last


def kernel(sizes, start, x_hbm, basis, scaled, x, xt, gath, y, part, sum1, sum2, got1, got2, got3, aug, inner,
           mine, mgot1, mgot2, mgot3, mall, tbuf, xsem, gs, gr, ss, sr, ms, mr, ts, tr):
    blk = lax.axis_index("blk")
    smp = lax.axis_index("smp")
    at = [smp // 16, lax.rem(smp // 4, 4), lax.rem(smp, 4)]

    def peer(axis, pos):
        where = list(at)
        where[axis] = pos
        return (blk, where[0] * 16 + where[1] * 4 + where[2])

    load = pltpu.make_async_copy(x_hbm, x, xsem)
    load.start()
    barrier = pltpu.get_barrier_semaphore()
    for axis in range(3):
        for d in (1, 2, 3):
            pl.semaphore_signal(barrier, inc=1, device_id=peer(axis, lax.rem(at[axis] + d, 4)), device_id_type=MESH)
    pl.semaphore_signal(barrier, inc=1, device_id=(1 - blk, smp), device_id_type=MESH)

    size = sizes[0]
    live = lax.broadcasted_iota(jnp.int32, (32, 256), 0) + smp * 32 < size

    def put_own(buf, rows):
        high = rows.astype(BF16)
        low = (rows - high.astype(F32)).astype(BF16)
        for i, v in enumerate((high[:, :128], high[:, 128:], low[:, :128], low[:, 128:])):
            buf[at[0], at[1], at[2], 32 * i : 32 * i + 32, :] = v

    put_own(gath.at[0], jnp.where(live, start[0], 0.0))
    pl.semaphore_wait(barrier, 10)

    def copies(src, dst, send, recv, axis):
        out = []
        for d in (1, 2, 3):
            pos = lax.rem(at[axis] + d, 4)
            c = pltpu.make_async_remote_copy(
                src_ref=src(pos), dst_ref=dst(d), send_sem=send.at[d - 1], recv_sem=recv.at[d - 1],
                device_id=peer(axis, pos), device_id_type=MESH,
            )
            c.start()
            out.append(c)
        return out

    def gather(phase):
        buf = gath.at[phase % 2]
        for stage in range(3):
            running = []
            for c, order in enumerate(ORDERS):
                r0, n = GATHER_ROWS[c]
                known = order[:stage]
                idx = tuple(slice(None) if a in known else at[a] for a in range(3)) + (pl.ds(r0, n),)
                view = buf.at[idx]
                running.append(copies(lambda pos: view, lambda d: view, gs.at[phase, c, stage], gr.at[phase, c, stage], order[stage]))
            yield
            for cs in running:
                for k in cs:
                    k.wait()

    def halves(buf):
        full = buf[...]
        p = [full[:, :, :, 32 * i : 32 * i + 32, :].reshape(CAP, 128) for i in range(4)]
        return jnp.concatenate(p[:2], axis=1), jnp.concatenate(p[2:], axis=1)

    def project(phase):
        @pl.loop(0, 4)
        def _(m):
            rows = pl.ds(pl.multiple_of(m * 256, 256), 256)
            high, low = halves(gath.at[phase])
            t = jnp.dot(x[rows, :], high, preferred_element_type=F32) + jnp.dot(x[rows, :], low, preferred_element_type=F32)
            th = t.astype(BF16)
            y[rows, 0:256] = th
            y[rows, 256:512] = (t - th.astype(F32)).astype(BF16)

    def expand():
        @pl.loop(0, 8)
        def _(m):
            rows = pl.ds(pl.multiple_of(m * 256, 256), 256)
            t = jnp.dot(xt[rows, :], y[:, 0:256], preferred_element_type=F32)
            t = t + jnp.dot(xt[rows, :], y[:, 256:512], preferred_element_type=F32)
            y0 = 2 * lax.rem(m, 2)
            part[m // 2, pl.ds(y0, 2), :, 0:32, :] = t[:, :128].reshape(2, 4, 32, 128)
            part[m // 2, pl.ds(y0, 2), :, 32:64, :] = t[:, 128:].reshape(2, 4, 32, 128)

    def pick(axis_index, n, pos):
        return tuple(pos if i == axis_index else slice(None) for i in range(n))

    def scatter(phase, result):
        running = []
        for c, (a1, a2, a3) in enumerate(ORDERS):
            rows = (pl.ds(*SUM_ROWS[c]),)
            running.append(copies(
                lambda pos: part.at[pick(a1, 3, pos) + rows], lambda d: got1.at[(d - 1, slice(None), slice(None)) + rows],
                ss.at[phase, c, 0], sr.at[phase, c, 0], a1))
        yield
        running2 = []
        for c, (a1, a2, a3) in enumerate(ORDERS):
            r0, n = SUM_ROWS[c]
            for k in running[c]:
                k.wait()
            v = part[pick(a1, 3, at[a1]) + (slice(r0, r0 + n),)]
            for d in range(3):
                v = v + got1[d, :, :, r0 : r0 + n, :]
            sum1[:, :, r0 : r0 + n, :] = v
            i2 = [a for a in range(3) if a != a1].index(a2)
            rows = (pl.ds(r0, n),)
            running2.append(copies(
                lambda pos: sum1.at[pick(i2, 2, pos) + rows], lambda d: got2.at[(d - 1, slice(None)) + rows],
                ss.at[phase, c, 1], sr.at[phase, c, 1], a2))
        yield
        running3 = []
        for c, (a1, a2, a3) in enumerate(ORDERS):
            r0, n = SUM_ROWS[c]
            for k in running2[c]:
                k.wait()
            i2 = [a for a in range(3) if a != a1].index(a2)
            v = sum1[pick(i2, 2, at[a2]) + (slice(r0, r0 + n),)]
            for d in range(3):
                v = v + got2[d, :, r0 : r0 + n, :]
            sum2[:, r0 : r0 + n, :] = v
            rows = pl.ds(r0, n)
            running3.append(copies(
                lambda pos: sum2.at[pos, rows], lambda d: got3.at[d - 1, rows],
                ss.at[phase, c, 2], sr.at[phase, c, 2], a3))
        yield
        pieces = []
        for c, (a1, a2, a3) in enumerate(ORDERS):
            r0, n = SUM_ROWS[c]
            for k in running3[c]:
                k.wait()
            v = sum2[at[a3], r0 : r0 + n, :]
            for d in range(3):
                v = v + got3[d, r0 : r0 + n, :]
            pieces.append(v)
        v = jnp.concatenate(pieces, axis=0)
        v = jnp.concatenate([v[:32], v[32:]], axis=1)
        result.append(jnp.where(live, v * (1.0 / (64 * 1024)), 0.0))

    def square(phase):
        high, low = halves(gath.at[phase])
        first, last = symmetric(high, low)
        cross = first[:, 256:512]
        return first[:, 0:256] + (cross + cross.T) + last

    def run(gen):
        for _ in gen:
            pass

    g = gather(0)
    next(g)
    load.wait()

    @pl.loop(0, 8)
    def _(m):
        cols = pl.ds(pl.multiple_of(m * 256, 256), 256)
        xt[cols, :] = x[:, cols].T

    run(g)
    project(0)
    expand()
    out = []
    run(scatter(0, out))
    put_own(gath.at[1], out[0])
    run(gather(1))
    project(1)
    expand()
    out = []
    s = scatter(1, out)
    next(s)
    factor_start(aug, square(1))
    factor_quarter(aug, 0)
    factor_quarter(aug, 1)
    next(s)
    factor_quarter(aug, 2)
    next(s)
    factor_quarter(aug, 3)
    run(s)
    image = exact(out[0], aug[:, 256:512], ((1,), (1,)))
    put_own(gath.at[0], image)
    run(gather(2))
    project(0)

    first, last = symmetric(y[:, 0:256], y[:, 256:512])
    cross = first[:, 256:512]
    total = (first[:, 0:256] + (cross + cross.T) + last) * (1.0 / (64 * 1024))
    for c, (r, q) in enumerate(((0, 0), (0, 128), (128, 128))):
        mine[c] = total[r : r + 128, q : q + 128].reshape(4, 32, 128)
    running = [copies(lambda pos: mine.at[c, pos], lambda d: mgot1.at[c, d - 1], ms.at[c, 0], mr.at[c, 0], o[0]) for c, o in enumerate(ORDERS)]
    factor_start(aug, square(0))
    factor_quarter(aug, 0)
    for stage, (had, now) in ((1, (None, mgot2)), (2, (mgot2, mgot3)), (3, (mgot3, mall))):
        after = []
        for c, o in enumerate(ORDERS):
            for k in running[c]:
                k.wait()
            if stage == 1:
                v = mine[c, at[o[0]]] + mgot1[c, 0] + mgot1[c, 1] + mgot1[c, 2]
            else:
                v = had[c, 0] + had[c, 1] + had[c, 2] + had[c, 3]
            axis = o[stage] if stage < 3 else o[0]
            now[c, at[axis]] = v
            view = now.at[c, at[axis]]
            after.append(copies(lambda pos: view, lambda d: view, ms.at[c, stage], mr.at[c, stage], axis))
        running = after
        factor_quarter(aug, stage)
    low = aug[:, 256:512]
    basis[0] = exact(image, low, ((1,), (1,))) * math.sqrt(CAP)
    for cs in running:
        for k in cs:
            k.wait()
    b00, b01, b11 = (mall[c].reshape(128, 128) for c in range(3))
    full = jnp.concatenate([jnp.concatenate([b00, b01], axis=1), jnp.concatenate([b01.T, b11], axis=1)], axis=0)
    ray = exact(exact(low, full, ((1,), (0,))), low, ((1,), (1,)))
    r = lax.broadcasted_iota(jnp.int32, (K, K), 0)
    q = lax.broadcasted_iota(jnp.int32, (K, K), 1)
    trace = jnp.sum(jnp.where(r == q, ray, 0.0), axis=(0, 1), keepdims=True)
    tbuf[0] = jnp.broadcast_to(trace, (8, 128))
    c = pltpu.make_async_remote_copy(
        src_ref=tbuf.at[0], dst_ref=tbuf.at[1], send_sem=ts, recv_sem=tr, device_id=(1 - blk, smp), device_id_type=MESH
    )
    c.start()
    c.wait()
    both = tbuf[0, 0:1, 0:1] + tbuf[1, 0:1, 0:1]
    scaled[0] = ray * (2.0 * K) / both


def body(genotypes, sizes, start):
    vm = pltpu.VMEM
    dma = pltpu.SemaphoreType.DMA
    return pl.pallas_call(
        kernel,
        out_shape=(jax.ShapeDtypeStruct((1, 32, K), F32), jax.ShapeDtypeStruct((1, K, K), F32)),
        in_specs=[
            pl.BlockSpec(memory_space=pltpu.SMEM),
            pl.BlockSpec(memory_space=pltpu.VMEM),
            pl.BlockSpec(memory_space=pl.ANY),
        ],
        out_specs=(pl.BlockSpec(memory_space=pltpu.VMEM), pl.BlockSpec(memory_space=pltpu.VMEM)),
        scratch_shapes=[
            vm((1024, CAP), BF16),
            vm((CAP, 1024), BF16),
            vm((2, 4, 4, 4, 128, 128), BF16),
            vm((1024, 512), BF16),
            vm((4, 4, 4, 64, 128), F32),
            vm((4, 4, 64, 128), F32),
            vm((4, 64, 128), F32),
            vm((3, 4, 4, 64, 128), F32),
            vm((3, 4, 64, 128), F32),
            vm((3, 64, 128), F32),
            vm((K, 2 * K), F32),
            vm((K, K), F32),
            vm((3, 4, 32, 128), F32),
            vm((3, 3, 32, 128), F32),
            vm((3, 4, 32, 128), F32),
            vm((3, 4, 32, 128), F32),
            vm((3, 4, 32, 128), F32),
            vm((2, 8, 128), F32),
            dma,
            dma((3, 3, 3, 3)),
            dma((3, 3, 3, 3)),
            dma((2, 3, 3, 3)),
            dma((2, 3, 3, 3)),
            dma((3, 4, 3)),
            dma((3, 4, 3)),
            dma,
            dma,
        ],
        compiler_params=pltpu.CompilerParams(
            collective_id=0, has_side_effects=True, vmem_limit_bytes=60 * 2**20
        ),
    )(sizes, start, genotypes.reshape(genotypes.shape[1:]))


def solution(mesh):
    return jax.shard_map(
        body,
        mesh=mesh,
        in_specs=(P("blk", "smp", None), P("blk"), P("blk", "smp", None)),
        out_specs=(P("blk", "smp", None), P("blk", None, None)),
        check_vma=False,
    )
```

```python
import functools
import math

import jax
import jax.numpy as jnp
from jax import lax
from jax.experimental import pallas as pl
from jax.experimental.pallas import tpu as pltpu
from jax.sharding import PartitionSpec as P

CAP = 2048
K = 256
F32 = jnp.float32
BF16 = jnp.bfloat16
MESH = pl.DeviceIdType.MESH
OTHERS = ((1, 2), (0, 2), (0, 1))
ORDERS = ((0, 1, 2), (1, 2, 0), (2, 0, 1))
SUM_ROWS = ((0, 24), (24, 24), (48, 16))
GATHER_ROWS = ((0, 48), (48, 48), (96, 32))


def split3(v):
    high = v.astype(BF16).astype(F32)
    rest = v - high
    middle = rest.astype(BF16).astype(F32)
    return high, middle, rest - middle


def exact(a, b, dims):
    return lax.dot_general(
        a, b, (dims, ((), ())), precision=lax.Precision.HIGHEST, preferred_element_type=F32
    )


def spread(block, first):
    return [jnp.broadcast_to(block[:, first + s : first + s + 1], (8, 128)) for s in range(8)]


def row_of(v, t):
    return jnp.broadcast_to(v[t : t + 1, :], v.shape)


def total(terms):
    terms = list(terms)
    while len(terms) > 1:
        terms = [terms[i] + terms[i + 1] if i + 1 < len(terms) else terms[i] for i in range(0, len(terms), 2)]
    return terms[0]


def factor8(columns):
    a = {(t, s): row_of(columns[s], t) for s in range(8) for t in range(s, 8)}
    inv = []
    for s in range(8):
        r = lax.rsqrt(a[s, s])
        inv.append(r)
        for t in range(s + 1, 8):
            a[t, s] = a[t, s] * r
        for t in range(s + 1, 8):
            for u in range(s + 1, t + 1):
                a[t, u] = a[t, u] - a[t, s] * a[u, s]
    w = {}
    for s in range(8):
        w[s, s] = inv[s]
        for t in range(s + 1, 8):
            acc = a[t, s] * w[s, s]
            for u in range(s + 1, t):
                acc = acc + a[t, u] * w[u, s]
            w[t, s] = -acc * inv[t]
    return w


def stack_rows(w):
    sub = lax.broadcasted_iota(jnp.int32, (8, 128), 0)
    columns = []
    for s in range(8):
        col = jnp.where(sub == s, w[s, s], 0.0)
        for t in range(s + 1, 8):
            col = jnp.where(sub == t, w[t, s], col)
        columns.append(wide(col))
    return columns


def wide(col):
    return jnp.concatenate([col] * 3, axis=1)


def six(v, right):
    a, b, c = split3(v)
    return jnp.concatenate([a, b, a, b, c, a] if right else [a, a, b, b, a, c], axis=0).astype(BF16)


TALL = (((0,), (0,)), ((), ()))


def factor_pair(aug, half, g):
    f = half * 128
    row = pl.multiple_of(f + g * 16, 16)
    next_row = pl.multiple_of(row + 8, 8)
    p1 = aug[pl.ds(row, 8), f : f + 384]
    p2 = aug[pl.ds(next_row, 8), f : f + 384]
    shift = lax.rem(128 - g * 16, 128)
    b1 = pltpu.roll(p1[:, 0:128], shift, 1)
    b2 = pltpu.roll(p2[:, 0:128], shift, 1)
    w1 = factor8(spread(b1, 0))
    cross = spread(b2, 0)
    low = [total(cross[k] * w1[s, k] for k in range(s + 1)) for s in range(8)]
    back = [total(low[s] * w1[s, k] for s in range(k, 8)) for k in range(8)]
    b2 = b2 - total(back[k] * row_of(b1, k) for k in range(8))
    w2 = factor8(spread(b2, 8))
    c1 = stack_rows(w1)
    rows1 = [row_of(p1, k) for k in range(8)]
    u1 = total(c1[k] * rows1[k] for k in range(8))
    p2 = p2 - total(wide(back[k]) * rows1[k] for k in range(8))
    c2 = stack_rows(w2)
    u2 = total(c2[k] * row_of(p2, k) for k in range(8))
    aug[pl.ds(row, 8), f : f + 384] = u1
    aug[pl.ds(next_row, 8), f : f + 384] = u2
    u = jnp.concatenate([u1, u2], axis=0)
    left = u[:, 0:128]
    lane = lax.broadcasted_iota(jnp.int32, left.shape, 1)
    left = jnp.where(lane > g * 16 + 15, left, 0.0)
    update = lax.dot_general(six(left, False), six(u, True), TALL, preferred_element_type=F32)
    aug[f : f + 128, f : f + 384] = aug[f : f + 128, f : f + 384] - update


def factor_start(aug, inner):
    aug[:, 0:256] = inner
    r = lax.broadcasted_iota(jnp.int32, (256, 256), 0)
    c = lax.broadcasted_iota(jnp.int32, (256, 256), 1)
    aug[:, 256:512] = jnp.where(r == c, 1.0, 0.0).astype(F32)


def factor_part(aug, first, count):
    @pl.loop(first % 8, first % 8 + count)
    def _(g):
        factor_pair(aug, first // 8, g)

    if first + count == 8:
        aug[128:256, 128:384] = aug[128:256, 128:384] - exact(aug[0:128, 128:256], aug[0:128, 128:384], ((0,), (0,)))


def symmetric(high, low):
    tall = (((0,), (0,)), ((), ()))
    first = lax.dot_general(high, jnp.concatenate([high, low], axis=1), tall, preferred_element_type=F32)
    last = lax.dot_general(low, low, tall, preferred_element_type=F32)
    return first, last


def kernel(sizes, start, x_hbm, basis, scaled, x, xt, gath, y, part, sum1, got1, got2, aug,
           mine, mgot1, mgot2, mgot3, mall, tbuf, xsem, gs, gr, ls, lr, ms, mr, ts, tr):
    blk = lax.axis_index("blk")
    smp = lax.axis_index("smp")
    at = [smp // 16, lax.rem(smp // 4, 4), lax.rem(smp, 4)]

    def peer(axis, pos):
        where = list(at)
        where[axis] = pos
        return (blk, where[0] * 16 + where[1] * 4 + where[2])

    load = pltpu.make_async_copy(x_hbm, x, xsem)
    load.start()
    barrier = pltpu.get_barrier_semaphore()
    steps = [(dz, dy, dx) for dz in range(4) for dy in range(4) for dx in range(4) if 0 < (dz > 0) + (dy > 0) + (dx > 0) < 3]
    for step in steps:
        z, y_, x_ = (lax.rem(p + d, 4) for p, d in zip(at, step))
        pl.semaphore_signal(barrier, inc=1, device_id=(blk, z * 16 + y_ * 4 + x_), device_id_type=MESH)
    pl.semaphore_signal(barrier, inc=1, device_id=(1 - blk, smp), device_id_type=MESH)

    size = sizes[0]
    live = lax.broadcasted_iota(jnp.int32, (32, 256), 0) + smp * 32 < size

    def put_own(buf, rows):
        high = rows.astype(BF16)
        low = (rows - high.astype(F32)).astype(BF16)
        for i, v in enumerate((high[:, :128], high[:, 128:], low[:, :128], low[:, 128:])):
            buf[at[0], at[1], at[2], 32 * i : 32 * i + 32, :] = v

    put_own(gath.at[0], jnp.where(live, start[0], 0.0))
    pl.semaphore_wait(barrier, len(steps) + 1)

    def copies(src, dst, send, recv, axis):
        out = []
        for d in (1, 2, 3):
            pos = lax.rem(at[axis] + d, 4)
            c = pltpu.make_async_remote_copy(
                src_ref=src(pos), dst_ref=dst(d), send_sem=send.at[d - 1], recv_sem=recv.at[d - 1],
                device_id=peer(axis, pos), device_id_type=MESH,
            )
            c.start()
            out.append(c)
        return out

    def pick(axis_index, n, pos):
        return tuple(pos if i == axis_index else slice(None) for i in range(n))

    def place(c, pc, pu, rest=()):
        idx = [slice(None)] * 3
        idx[c], idx[OTHERS[c][0]] = pc, pu
        return tuple(idx) + rest

    def plane_copy(c, du, dv, src, dst, send, recv):
        u, v = OTHERS[c]
        where = list(at)
        where[u] = lax.rem(at[u] + du, 4)
        where[v] = lax.rem(at[v] + dv, 4)
        k = pltpu.make_async_remote_copy(
            src_ref=src, dst_ref=dst, send_sem=send.at[4 * du + dv - 1], recv_sem=recv.at[4 * du + dv - 1],
            device_id=(blk, where[0] * 16 + where[1] * 4 + where[2]), device_id_type=MESH,
        )
        k.start()
        return k

    def wait_all(running):
        for cs in running:
            for k in cs:
                k.wait()

    def gather(phase):
        buf = gath.at[phase % 2]
        short, long = {}, []
        for du in (2, 1, 3, 0):
            for c in range(3):
                view = buf.at[at[0], at[1], at[2], pl.ds(*GATHER_ROWS[c])]
                for dv in range(4):
                    if du + dv:
                        short[c, du, dv] = plane_copy(c, du, dv, view, view, gs.at[phase, c], gr.at[phase, c])
        yield
        for du in (0, 1, 3, 2):
            for c in range(3):
                for dv in range(4):
                    if du + dv:
                        short[c, du, dv].wait_recv()
                line = lax.rem(at[OTHERS[c][0]] + 4 - du, 4)
                view = buf.at[place(c, at[c], line, (pl.ds(*GATHER_ROWS[c]),))]
                long.append(copies(lambda pos: view, lambda d: view, ls.at[phase, c, du], lr.at[phase, c, du], c))
        for k in short.values():
            k.wait_send()
        wait_all(long)

    def halves(buf):
        full = buf[...]
        p = [full[:, :, :, 32 * i : 32 * i + 32, :].reshape(CAP, 128) for i in range(4)]
        return jnp.concatenate(p[:2], axis=1), jnp.concatenate(p[2:], axis=1)

    def project(phase):
        @pl.loop(0, 2)
        def _(m):
            rows = pl.ds(pl.multiple_of(m * 512, 512), 512)
            high, low = halves(gath.at[phase])
            t = jnp.dot(x[rows, :], high, preferred_element_type=F32) + jnp.dot(x[rows, :], low, preferred_element_type=F32)
            th = t.astype(BF16)
            y[rows, 0:256] = th
            y[rows, 256:512] = (t - th.astype(F32)).astype(BF16)

    def expand():
        @pl.loop(0, 4)
        def _(m):
            rows = pl.ds(pl.multiple_of(m * 512, 512), 512)
            t = jnp.dot(xt[rows, :], y[:, 0:256], preferred_element_type=F32)
            t = t + jnp.dot(xt[rows, :], y[:, 256:512], preferred_element_type=F32)
            part[m, :, :, 0:32, :] = t[:, :128].reshape(4, 4, 32, 128)
            part[m, :, :, 32:64, :] = t[:, 128:].reshape(4, 4, 32, 128)

    def scatter(phase, result):
        long, short = {}, {}
        for du in (2, 1, 3, 0):
            for c in range(3):
                rows = (pl.ds(*SUM_ROWS[c]),)
                line = lax.rem(at[OTHERS[c][0]] + du, 4)
                long[c, du] = copies(
                    lambda pos: part.at[place(c, pos, line, rows)], lambda d: got1.at[(d - 1, du, slice(None)) + rows],
                    ls.at[3 + phase, c, du], lr.at[3 + phase, c, du], c)
        yield
        for du in (2, 1, 3, 0):
            for c in range(3):
                r0, n = SUM_ROWS[c]
                for k in long[c, du]:
                    k.wait_recv()
                line = lax.rem(at[OTHERS[c][0]] + du, 4)
                v = part[place(c, at[c], line, (slice(r0, r0 + n),))]
                for d in range(3):
                    v = v + got1[d, du, :, r0 : r0 + n, :]
                sum1[du, :, r0 : r0 + n, :] = v
                for dv in range(4):
                    if du + dv:
                        pv = lax.rem(at[OTHERS[c][1]] + dv, 4)
                        short[c, du, dv] = plane_copy(
                            c, du, dv, sum1.at[du, pv, pl.ds(r0, n)], got2.at[4 * du + dv - 1, pl.ds(r0, n)],
                            gs.at[3 + phase, c], gr.at[3 + phase, c])
            yield
        for k in [k for ks in long.values() for k in ks]:
            k.wait_send()
        pieces = []
        for c in range(3):
            r0, n = SUM_ROWS[c]
            v = sum1[0, at[OTHERS[c][1]], r0 : r0 + n, :]
            for du in (2, 1, 3, 0):
                for dv in range(4):
                    if du + dv:
                        short[c, du, dv].wait()
                        v = v + got2[4 * du + dv - 1, r0 : r0 + n, :]
            pieces.append(v)
        v = jnp.concatenate(pieces, axis=0)
        v = jnp.concatenate([v[:32], v[32:]], axis=1)
        result.append(jnp.where(live, v * (1.0 / (64 * 1024)), 0.0))

    def square(phase):
        high, low = halves(gath.at[phase])
        first, last = symmetric(high, low)
        cross = first[:, 256:512]
        return first[:, 0:256] + (cross + cross.T) + last

    def run(gen):
        for _ in gen:
            pass

    g = gather(0)
    next(g)
    load.wait()

    @pl.loop(0, 8)
    def _(m):
        cols = pl.ds(pl.multiple_of(m * 256, 256), 256)
        xt[cols, :] = x[:, cols].T

    run(g)
    project(0)
    expand()
    out = []
    run(scatter(0, out))
    put_own(gath.at[1], out[0])
    run(gather(1))
    project(1)
    expand()
    out = []
    s = scatter(1, out)
    next(s)
    factor_start(aug, square(1))
    factor_part(aug, 0, 4)
    next(s)
    factor_part(aug, 4, 2)
    next(s)
    factor_part(aug, 6, 2)
    next(s)
    factor_part(aug, 8, 2)
    next(s)
    factor_part(aug, 10, 6)
    run(s)
    image = exact(out[0], aug[:, 256:512], ((1,), (1,)))
    put_own(gath.at[0], image)
    run(gather(2))
    project(0)

    first, last = symmetric(y[:, 0:256], y[:, 256:512])
    cross = first[:, 256:512]
    total = (first[:, 0:256] + (cross + cross.T) + last) * (1.0 / (64 * 1024))
    for c, (r, q) in enumerate(((0, 0), (0, 128), (128, 128))):
        mine[c] = total[r : r + 128, q : q + 128].reshape(4, 32, 128)
    running = [copies(lambda pos: mine.at[c, pos], lambda d: mgot1.at[c, d - 1], ms.at[c, 0], mr.at[c, 0], o[0]) for c, o in enumerate(ORDERS)]
    factor_start(aug, square(0))
    factor_part(aug, 0, 4)
    for stage, (had, now) in ((1, (None, mgot2)), (2, (mgot2, mgot3)), (3, (mgot3, mall))):
        after = []
        for c, o in enumerate(ORDERS):
            for k in running[c]:
                k.wait()
            if stage == 1:
                v = mine[c, at[o[0]]] + mgot1[c, 0] + mgot1[c, 1] + mgot1[c, 2]
            else:
                v = had[c, 0] + had[c, 1] + had[c, 2] + had[c, 3]
            axis = o[stage] if stage < 3 else o[0]
            now[c, at[axis]] = v
            view = now.at[c, at[axis]]
            after.append(copies(lambda pos: view, lambda d: view, ms.at[c, stage], mr.at[c, stage], axis))
        running = after
        factor_part(aug, 4 * stage, 4)
    low = aug[:, 256:512]
    basis[0] = exact(image, low, ((1,), (1,))) * math.sqrt(CAP)
    for cs in running:
        for k in cs:
            k.wait()
    b00, b01, b11 = (mall[c].reshape(128, 128) for c in range(3))
    full = jnp.concatenate([jnp.concatenate([b00, b01], axis=1), jnp.concatenate([b01.T, b11], axis=1)], axis=0)
    ray = exact(exact(low, full, ((1,), (0,))), low, ((1,), (1,)))
    r = lax.broadcasted_iota(jnp.int32, (K, K), 0)
    q = lax.broadcasted_iota(jnp.int32, (K, K), 1)
    trace = jnp.sum(jnp.where(r == q, ray, 0.0), axis=(0, 1), keepdims=True)
    tbuf[0] = jnp.broadcast_to(trace, (8, 128))
    c = pltpu.make_async_remote_copy(
        src_ref=tbuf.at[0], dst_ref=tbuf.at[1], send_sem=ts, recv_sem=tr, device_id=(1 - blk, smp), device_id_type=MESH
    )
    c.start()
    c.wait()
    both = tbuf[0, 0:1, 0:1] + tbuf[1, 0:1, 0:1]
    scaled[0] = ray * (2.0 * K) / both


def body(genotypes, sizes, start):
    vm = pltpu.VMEM
    dma = pltpu.SemaphoreType.DMA
    return pl.pallas_call(
        kernel,
        out_shape=(jax.ShapeDtypeStruct((1, 32, K), F32), jax.ShapeDtypeStruct((1, K, K), F32)),
        in_specs=[
            pl.BlockSpec(memory_space=pltpu.SMEM),
            pl.BlockSpec(memory_space=pltpu.VMEM),
            pl.BlockSpec(memory_space=pl.ANY),
        ],
        out_specs=(pl.BlockSpec(memory_space=pltpu.VMEM), pl.BlockSpec(memory_space=pltpu.VMEM)),
        scratch_shapes=[
            vm((1024, CAP), BF16),
            vm((CAP, 1024), BF16),
            vm((2, 4, 4, 4, 128, 128), BF16),
            vm((1024, 512), BF16),
            vm((4, 4, 4, 64, 128), F32),
            vm((4, 4, 64, 128), F32),
            vm((3, 4, 4, 64, 128), F32),
            vm((15, 64, 128), F32),
            vm((K, 2 * K), F32),
            vm((3, 4, 32, 128), F32),
            vm((3, 3, 32, 128), F32),
            vm((3, 4, 32, 128), F32),
            vm((3, 4, 32, 128), F32),
            vm((3, 4, 32, 128), F32),
            vm((2, 8, 128), F32),
            dma,
            dma((5, 3, 15)),
            dma((5, 3, 15)),
            dma((5, 3, 4, 3)),
            dma((5, 3, 4, 3)),
            dma((3, 4, 3)),
            dma((3, 4, 3)),
            dma,
            dma,
        ],
        compiler_params=pltpu.CompilerParams(
            collective_id=0, has_side_effects=True, vmem_limit_bytes=60 * 2**20
        ),
    )(sizes, start, genotypes.reshape(genotypes.shape[1:]))


def solution(mesh):
    return jax.shard_map(
        body,
        mesh=mesh,
        in_specs=(P("blk", "smp", None), P("blk"), P("blk", "smp", None)),
        out_specs=(P("blk", "smp", None), P("blk", None, None)),
        check_vma=False,
    )
```

```python
import functools
import math

import jax
import jax.numpy as jnp
from jax import lax
from jax.experimental import pallas as pl
from jax.experimental.pallas import tpu as pltpu
from jax.sharding import PartitionSpec as P

CAP = 2048
K = 256
F32 = jnp.float32
BF16 = jnp.bfloat16
MESH = pl.DeviceIdType.MESH
OTHERS = ((1, 2), (0, 2), (0, 1))
ORDERS = ((0, 1, 2), (1, 2, 0), (2, 0, 1))
SUM_ROWS = ((0, 24), (24, 24), (48, 16))
GATHER_ROWS = ((0, 48), (48, 48), (96, 32))


def split3(v):
    high = v.astype(BF16).astype(F32)
    rest = v - high
    middle = rest.astype(BF16).astype(F32)
    return high, middle, rest - middle


def exact(a, b, dims):
    return lax.dot_general(
        a, b, (dims, ((), ())), precision=lax.Precision.HIGHEST, preferred_element_type=F32
    )


def spread(block, first):
    return [jnp.broadcast_to(block[:, first + s : first + s + 1], (8, 128)) for s in range(8)]


def row_of(v, t):
    return jnp.broadcast_to(v[t : t + 1, :], v.shape)


def total(terms):
    terms = list(terms)
    while len(terms) > 1:
        terms = [terms[i] + terms[i + 1] if i + 1 < len(terms) else terms[i] for i in range(0, len(terms), 2)]
    return terms[0]


def factor8(columns):
    a = {(t, s): row_of(columns[s], t) for s in range(8) for t in range(s, 8)}
    inv = []
    for s in range(8):
        r = lax.rsqrt(a[s, s])
        inv.append(r)
        for t in range(s + 1, 8):
            a[t, s] = a[t, s] * r
        for t in range(s + 1, 8):
            for u in range(s + 1, t + 1):
                a[t, u] = a[t, u] - a[t, s] * a[u, s]
    w = {}
    for s in range(8):
        w[s, s] = inv[s]
        for t in range(s + 1, 8):
            acc = a[t, s] * w[s, s]
            for u in range(s + 1, t):
                acc = acc + a[t, u] * w[u, s]
            w[t, s] = -acc * inv[t]
    return w


def stack_rows(w):
    sub = lax.broadcasted_iota(jnp.int32, (8, 128), 0)
    columns = []
    for s in range(8):
        col = jnp.where(sub == s, w[s, s], 0.0)
        for t in range(s + 1, 8):
            col = jnp.where(sub == t, w[t, s], col)
        columns.append(wide(col))
    return columns


def wide(col):
    return jnp.concatenate([col] * 3, axis=1)


def six(v, right):
    a, b, c = split3(v)
    return jnp.concatenate([a, b, a, b, c, a] if right else [a, a, b, b, a, c], axis=0).astype(BF16)


TALL = (((0,), (0,)), ((), ()))


def factor_pair(aug, half, g):
    f = half * 128
    row = pl.multiple_of(f + g * 16, 16)
    next_row = pl.multiple_of(row + 8, 8)
    p1 = aug[pl.ds(row, 8), f : f + 384]
    p2 = aug[pl.ds(next_row, 8), f : f + 384]
    shift = lax.rem(128 - g * 16, 128)
    b1 = pltpu.roll(p1[:, 0:128], shift, 1)
    b2 = pltpu.roll(p2[:, 0:128], shift, 1)
    w1 = factor8(spread(b1, 0))
    cross = spread(b2, 0)
    low = [total(cross[k] * w1[s, k] for k in range(s + 1)) for s in range(8)]
    back = [total(low[s] * w1[s, k] for s in range(k, 8)) for k in range(8)]
    b2 = b2 - total(back[k] * row_of(b1, k) for k in range(8))
    w2 = factor8(spread(b2, 8))
    c1 = stack_rows(w1)
    rows1 = [row_of(p1, k) for k in range(8)]
    u1 = total(c1[k] * rows1[k] for k in range(8))
    p2 = p2 - total(wide(back[k]) * rows1[k] for k in range(8))
    c2 = stack_rows(w2)
    u2 = total(c2[k] * row_of(p2, k) for k in range(8))
    aug[pl.ds(row, 8), f : f + 384] = u1
    aug[pl.ds(next_row, 8), f : f + 384] = u2
    u = jnp.concatenate([u1, u2], axis=0)
    left = u[:, 0:128]
    lane = lax.broadcasted_iota(jnp.int32, left.shape, 1)
    left = jnp.where(lane > g * 16 + 15, left, 0.0)
    update = lax.dot_general(six(left, False), six(u, True), TALL, preferred_element_type=F32)
    aug[f : f + 128, f : f + 384] = aug[f : f + 128, f : f + 384] - update


def factor_start(aug, inner):
    aug[:, 0:256] = inner
    r = lax.broadcasted_iota(jnp.int32, (256, 256), 0)
    c = lax.broadcasted_iota(jnp.int32, (256, 256), 1)
    aug[:, 256:512] = jnp.where(r == c, 1.0, 0.0).astype(F32)


def factor_part(aug, first, count):
    @pl.loop(first % 8, first % 8 + count)
    def _(g):
        factor_pair(aug, first // 8, g)

    if first + count == 8:
        aug[128:256, 128:384] = aug[128:256, 128:384] - exact(aug[0:128, 128:256], aug[0:128, 128:384], ((0,), (0,)))


def symmetric(high, low):
    tall = (((0,), (0,)), ((), ()))
    first = lax.dot_general(high, jnp.concatenate([high, low], axis=1), tall, preferred_element_type=F32)
    last = lax.dot_general(low, low, tall, preferred_element_type=F32)
    return first, last


def kernel(sizes, start, x_hbm, basis, scaled, x, xt, gath, y, part, sum1, got1, got2, aug,
           mine, mgot1, mgot2, mgot3, mall, tbuf, xsem, gs, gr, ls, lr, ms, mr, ts, tr):
    blk = lax.axis_index("blk")
    smp = lax.axis_index("smp")
    at = [smp // 16, lax.rem(smp // 4, 4), lax.rem(smp, 4)]

    def peer(axis, pos):
        where = list(at)
        where[axis] = pos
        return (blk, where[0] * 16 + where[1] * 4 + where[2])

    load = pltpu.make_async_copy(x_hbm, x, xsem)
    load.start()
    barrier = pltpu.get_barrier_semaphore()
    steps = [(dz, dy, dx) for dz in range(4) for dy in range(4) for dx in range(4) if 0 < (dz > 0) + (dy > 0) + (dx > 0) < 3]
    for step in steps:
        z, y_, x_ = (lax.rem(p + d, 4) for p, d in zip(at, step))
        pl.semaphore_signal(barrier, inc=1, device_id=(blk, z * 16 + y_ * 4 + x_), device_id_type=MESH)
    pl.semaphore_signal(barrier, inc=1, device_id=(1 - blk, smp), device_id_type=MESH)

    size = sizes[0]
    live = lax.broadcasted_iota(jnp.int32, (32, 256), 0) + smp * 32 < size

    def put_own(buf, rows):
        high = rows.astype(BF16)
        low = (rows - high.astype(F32)).astype(BF16)
        for i, v in enumerate((high[:, :128], high[:, 128:], low[:, :128], low[:, 128:])):
            buf[at[0], at[1], at[2], 32 * i : 32 * i + 32, :] = v

    put_own(gath.at[0], jnp.where(live, start[0], 0.0))
    pl.semaphore_wait(barrier, len(steps) + 1)

    def copies(src, dst, send, recv, axis, ds=(1, 2, 3)):
        out = []
        for d in ds:
            pos = lax.rem(at[axis] + d, 4)
            c = pltpu.make_async_remote_copy(
                src_ref=src(pos), dst_ref=dst(d), send_sem=send.at[d - 1], recv_sem=recv.at[d - 1],
                device_id=peer(axis, pos), device_id_type=MESH,
            )
            c.start()
            out.append(c)
        return out

    def pick(axis_index, n, pos):
        return tuple(pos if i == axis_index else slice(None) for i in range(n))

    def place(c, pc, pu, rest=()):
        idx = [slice(None)] * 3
        idx[c], idx[OTHERS[c][0]] = pc, pu
        return tuple(idx) + rest

    def plane_copy(c, du, dv, src, dst, send, recv):
        u, v = OTHERS[c]
        where = list(at)
        where[u] = lax.rem(at[u] + du, 4)
        where[v] = lax.rem(at[v] + dv, 4)
        k = pltpu.make_async_remote_copy(
            src_ref=src, dst_ref=dst, send_sem=send.at[4 * du + dv - 1], recv_sem=recv.at[4 * du + dv - 1],
            device_id=(blk, where[0] * 16 + where[1] * 4 + where[2]), device_id_type=MESH,
        )
        k.start()
        return k

    def wait_all(running):
        for cs in running:
            for k in cs:
                k.wait()

    def gather(phase):
        buf = gath.at[phase % 2]
        short, long = {}, []
        for du in (0, 1, 3, 2):
            for c in range(3):
                view = buf.at[at[0], at[1], at[2], pl.ds(*GATHER_ROWS[c])]
                for dv in range(4):
                    if du + dv:
                        short[c, du, dv] = plane_copy(c, du, dv, view, view, gs.at[phase, c], gr.at[phase, c])
        yield
        for du in (0, 1, 3, 2):
            for c in range(3):
                for dv in range(4):
                    if du + dv:
                        short[c, du, dv].wait_recv()
                line = lax.rem(at[OTHERS[c][0]] + 4 - du, 4)
                view = buf.at[place(c, at[c], line, (pl.ds(*GATHER_ROWS[c]),))]
                long.append(copies(lambda pos: view, lambda d: view, ls.at[phase, c, du], lr.at[phase, c, du], c))
        for k in short.values():
            k.wait_send()
        wait_all(long)

    def halves(buf):
        full = buf[...]
        p = [full[:, :, :, 32 * i : 32 * i + 32, :].reshape(CAP, 128) for i in range(4)]
        return jnp.concatenate(p[:2], axis=1), jnp.concatenate(p[2:], axis=1)

    def project(phase):
        @pl.loop(0, 2)
        def _(m):
            rows = pl.ds(pl.multiple_of(m * 512, 512), 512)
            high, low = halves(gath.at[phase])
            t = jnp.dot(x[rows, :], high, preferred_element_type=F32) + jnp.dot(x[rows, :], low, preferred_element_type=F32)
            th = t.astype(BF16)
            y[rows, 0:256] = th
            y[rows, 256:512] = (t - th.astype(F32)).astype(BF16)

    def expand(z):
        @pl.loop(0, 2)
        def _(m):
            rows = pl.ds(pl.multiple_of(z * 512 + m * 256, 256), 256)
            t = jnp.dot(xt[rows, :], y[:, 0:256], preferred_element_type=F32)
            t = t + jnp.dot(xt[rows, :], y[:, 256:512], preferred_element_type=F32)
            part[z, pl.ds(2 * m, 2), :, 0:32, :] = t[:, :128].reshape(2, 4, 32, 128)
            part[z, pl.ds(2 * m, 2), :, 32:64, :] = t[:, 128:].reshape(2, 4, 32, 128)

    def scatter(phase, result):
        long, short = {(0, du): [] for du in range(4)}, {}

        def send(c, du, d):
            rows = (pl.ds(*SUM_ROWS[c]),)
            line = lax.rem(at[OTHERS[c][0]] + du, 4)
            long.setdefault((c, du), []).extend(copies(
                lambda pos: part.at[place(c, pos, line, rows)], lambda d: got1.at[(d - 1, du, slice(None)) + rows],
                ls.at[3 + phase, c, du], lr.at[3 + phase, c, du], c, d))

        for du in (2, 1, 3, 0):
            expand(lax.rem(at[0] + du, 4))
            for c in (1, 2):
                send(c, du, (1, 2, 3))
            if du:
                for line in (2, 1, 3, 0):
                    send(0, line, (du,))
        yield
        for du in (2, 1, 3, 0):
            for c in range(3):
                r0, n = SUM_ROWS[c]
                for k in long[c, du]:
                    k.wait_recv()
                line = lax.rem(at[OTHERS[c][0]] + du, 4)
                v = part[place(c, at[c], line, (slice(r0, r0 + n),))]
                for d in range(3):
                    v = v + got1[d, du, :, r0 : r0 + n, :]
                sum1[du, :, r0 : r0 + n, :] = v
                for dv in range(4):
                    if du + dv:
                        pv = lax.rem(at[OTHERS[c][1]] + dv, 4)
                        short[c, du, dv] = plane_copy(
                            c, du, dv, sum1.at[du, pv, pl.ds(r0, n)], got2.at[4 * du + dv - 1, pl.ds(r0, n)],
                            gs.at[3 + phase, c], gr.at[3 + phase, c])
            yield
        for k in [k for ks in long.values() for k in ks]:
            k.wait_send()
        pieces = []
        for c in range(3):
            r0, n = SUM_ROWS[c]
            v = sum1[0, at[OTHERS[c][1]], r0 : r0 + n, :]
            for du in (2, 1, 3, 0):
                for dv in range(4):
                    if du + dv:
                        short[c, du, dv].wait()
                        v = v + got2[4 * du + dv - 1, r0 : r0 + n, :]
            pieces.append(v)
        v = jnp.concatenate(pieces, axis=0)
        v = jnp.concatenate([v[:32], v[32:]], axis=1)
        result.append(jnp.where(live, v * (1.0 / (64 * 1024)), 0.0))

    def square(phase):
        high, low = halves(gath.at[phase])
        first, last = symmetric(high, low)
        cross = first[:, 256:512]
        return first[:, 0:256] + (cross + cross.T) + last

    def run(gen):
        for _ in gen:
            pass

    g = gather(0)
    next(g)
    load.wait()

    @pl.loop(0, 8)
    def _(m):
        cols = pl.ds(pl.multiple_of(m * 256, 256), 256)
        xt[cols, :] = x[:, cols].T

    run(g)
    project(0)
    out = []
    run(scatter(0, out))
    put_own(gath.at[1], out[0])
    run(gather(1))
    project(1)
    out = []
    s = scatter(1, out)
    next(s)
    factor_start(aug, square(1))
    factor_part(aug, 0, 4)
    next(s)
    factor_part(aug, 4, 2)
    next(s)
    factor_part(aug, 6, 2)
    next(s)
    factor_part(aug, 8, 2)
    next(s)
    factor_part(aug, 10, 6)
    run(s)
    image = exact(out[0], aug[:, 256:512], ((1,), (1,)))
    put_own(gath.at[0], image)
    run(gather(2))
    project(0)

    first, last = symmetric(y[:, 0:256], y[:, 256:512])
    cross = first[:, 256:512]
    total = (first[:, 0:256] + (cross + cross.T) + last) * (1.0 / (64 * 1024))
    for c, (r, q) in enumerate(((0, 0), (0, 128), (128, 128))):
        mine[c] = total[r : r + 128, q : q + 128].reshape(4, 32, 128)
    running = [copies(lambda pos: mine.at[c, pos], lambda d: mgot1.at[c, d - 1], ms.at[c, 0], mr.at[c, 0], o[0]) for c, o in enumerate(ORDERS)]
    factor_start(aug, square(0))
    factor_part(aug, 0, 4)
    for stage, (had, now) in ((1, (None, mgot2)), (2, (mgot2, mgot3)), (3, (mgot3, mall))):
        after = []
        for c, o in enumerate(ORDERS):
            for k in running[c]:
                k.wait()
            if stage == 1:
                v = mine[c, at[o[0]]] + mgot1[c, 0] + mgot1[c, 1] + mgot1[c, 2]
            else:
                v = had[c, 0] + had[c, 1] + had[c, 2] + had[c, 3]
            axis = o[stage] if stage < 3 else o[0]
            now[c, at[axis]] = v
            view = now.at[c, at[axis]]
            after.append(copies(lambda pos: view, lambda d: view, ms.at[c, stage], mr.at[c, stage], axis))
        running = after
        factor_part(aug, 4 * stage, 4)
    low = aug[:, 256:512]
    basis[0] = exact(image, low, ((1,), (1,))) * math.sqrt(CAP)
    for cs in running:
        for k in cs:
            k.wait()
    b00, b01, b11 = (mall[c].reshape(128, 128) for c in range(3))
    full = jnp.concatenate([jnp.concatenate([b00, b01], axis=1), jnp.concatenate([b01.T, b11], axis=1)], axis=0)
    left = exact(low, full, ((1,), (0,)))
    tbuf[0] = jnp.broadcast_to(jnp.sum(left * low, axis=(0, 1), keepdims=True), (8, 128))
    c = pltpu.make_async_remote_copy(
        src_ref=tbuf.at[0], dst_ref=tbuf.at[1], send_sem=ts, recv_sem=tr, device_id=(1 - blk, smp), device_id_type=MESH
    )
    c.start()
    ray = exact(left, low, ((1,), (1,)))
    c.wait()
    both = tbuf[0, 0:1, 0:1] + tbuf[1, 0:1, 0:1]
    scaled[0] = ray * (2.0 * K) / both


def hand_out(basis, scaled, basis_out, scaled_out):
    basis_out[...] = basis[...]
    scaled_out[...] = scaled[...]


def body(genotypes, sizes, start):
    vm = pltpu.VMEM
    dma = pltpu.SemaphoreType.DMA
    shapes = (jax.ShapeDtypeStruct((1, 32, K), F32), jax.ShapeDtypeStruct((1, K, K), F32))
    results = pl.pallas_call(
        kernel,
        out_shape=shapes,
        in_specs=[
            pl.BlockSpec(memory_space=pltpu.SMEM),
            pl.BlockSpec(memory_space=pltpu.VMEM),
            pl.BlockSpec(memory_space=pl.ANY),
        ],
        out_specs=(pl.BlockSpec(memory_space=pltpu.VMEM), pl.BlockSpec(memory_space=pltpu.VMEM)),
        scratch_shapes=[
            vm((1024, CAP), BF16),
            vm((CAP, 1024), BF16),
            vm((2, 4, 4, 4, 128, 128), BF16),
            vm((1024, 512), BF16),
            vm((4, 4, 4, 64, 128), F32),
            vm((4, 4, 64, 128), F32),
            vm((3, 4, 4, 64, 128), F32),
            vm((15, 64, 128), F32),
            vm((K, 2 * K), F32),
            vm((3, 4, 32, 128), F32),
            vm((3, 3, 32, 128), F32),
            vm((3, 4, 32, 128), F32),
            vm((3, 4, 32, 128), F32),
            vm((3, 4, 32, 128), F32),
            vm((2, 8, 128), F32),
            dma,
            dma((5, 3, 15)),
            dma((5, 3, 15)),
            dma((5, 3, 4, 3)),
            dma((5, 3, 4, 3)),
            dma((3, 4, 3)),
            dma((3, 4, 3)),
            dma,
            dma,
        ],
        compiler_params=pltpu.CompilerParams(
            collective_id=0, has_side_effects=True, vmem_limit_bytes=60 * 2**20
        ),
    )(sizes, start, genotypes.reshape(genotypes.shape[1:]))
    return pl.pallas_call(hand_out, out_shape=shapes)(*results)


def solution(mesh):
    return jax.shard_map(
        body,
        mesh=mesh,
        in_specs=(P("blk", "smp", None), P("blk"), P("blk", "smp", None)),
        out_specs=(P("blk", "smp", None), P("blk", None, None)),
        check_vma=False,
    )
```

```python
import functools
import math

import jax
import jax.numpy as jnp
from jax import lax
from jax.experimental import pallas as pl
from jax.experimental.pallas import tpu as pltpu
from jax.sharding import PartitionSpec as P

CAP = 2048
K = 256
F32 = jnp.float32
BF16 = jnp.bfloat16
MESH = pl.DeviceIdType.MESH
OTHERS = ((1, 2), (0, 2), (0, 1))
ORDERS = ((0, 1, 2), (1, 2, 0), (2, 0, 1))
SUM_ROWS = ((0, 24), (24, 24), (48, 16))
GATHER_ROWS = ((0, 48), (48, 48), (96, 32))


def split3(v):
    high = v.astype(BF16).astype(F32)
    rest = v - high
    middle = rest.astype(BF16).astype(F32)
    return high, middle, rest - middle


def exact(a, b, dims):
    return lax.dot_general(
        a, b, (dims, ((), ())), precision=lax.Precision.HIGHEST, preferred_element_type=F32
    )


def spread(block, first):
    return [jnp.broadcast_to(block[:, first + s : first + s + 1], (8, 128)) for s in range(8)]


def row_of(v, t):
    return jnp.broadcast_to(v[t : t + 1, :], v.shape)


def total(terms):
    terms = list(terms)
    while len(terms) > 1:
        terms = [terms[i] + terms[i + 1] if i + 1 < len(terms) else terms[i] for i in range(0, len(terms), 2)]
    return terms[0]


def factor8(columns):
    a = {(t, s): row_of(columns[s], t) for s in range(8) for t in range(s, 8)}
    inv = []
    for s in range(8):
        r = lax.rsqrt(a[s, s])
        inv.append(r)
        for t in range(s + 1, 8):
            a[t, s] = a[t, s] * r
        for t in range(s + 1, 8):
            for u in range(s + 1, t + 1):
                a[t, u] = a[t, u] - a[t, s] * a[u, s]
    w = {}
    for s in range(8):
        w[s, s] = inv[s]
        for t in range(s + 1, 8):
            acc = a[t, s] * w[s, s]
            for u in range(s + 1, t):
                acc = acc + a[t, u] * w[u, s]
            w[t, s] = -acc * inv[t]
    return w


def stack_rows(w):
    sub = lax.broadcasted_iota(jnp.int32, (8, 128), 0)
    columns = []
    for s in range(8):
        col = jnp.where(sub == s, w[s, s], 0.0)
        for t in range(s + 1, 8):
            col = jnp.where(sub == t, w[t, s], col)
        columns.append(wide(col))
    return columns


def wide(col):
    return jnp.concatenate([col] * 3, axis=1)


def six(v, right):
    a, b, c = split3(v)
    return jnp.concatenate([a, b, a, b, c, a] if right else [a, a, b, b, a, c], axis=0).astype(BF16)


TALL = (((0,), (0,)), ((), ()))


def factor_pair(aug, half, g):
    f = half * 128
    row = pl.multiple_of(f + g * 16, 16)
    next_row = pl.multiple_of(row + 8, 8)
    p1 = aug[pl.ds(row, 8), f : f + 384]
    p2 = aug[pl.ds(next_row, 8), f : f + 384]
    shift = lax.rem(128 - g * 16, 128)
    b1 = pltpu.roll(p1[:, 0:128], shift, 1)
    b2 = pltpu.roll(p2[:, 0:128], shift, 1)
    w1 = factor8(spread(b1, 0))
    cross = spread(b2, 0)
    low = [total(cross[k] * w1[s, k] for k in range(s + 1)) for s in range(8)]
    back = [total(low[s] * w1[s, k] for s in range(k, 8)) for k in range(8)]
    b2 = b2 - total(back[k] * row_of(b1, k) for k in range(8))
    w2 = factor8(spread(b2, 8))
    c1 = stack_rows(w1)
    rows1 = [row_of(p1, k) for k in range(8)]
    u1 = total(c1[k] * rows1[k] for k in range(8))
    p2 = p2 - total(wide(back[k]) * rows1[k] for k in range(8))
    c2 = stack_rows(w2)
    u2 = total(c2[k] * row_of(p2, k) for k in range(8))
    aug[pl.ds(row, 8), f : f + 384] = u1
    aug[pl.ds(next_row, 8), f : f + 384] = u2
    u = jnp.concatenate([u1, u2], axis=0)
    left = u[:, 0:128]
    lane = lax.broadcasted_iota(jnp.int32, left.shape, 1)
    left = jnp.where(lane > g * 16 + 15, left, 0.0)
    update = lax.dot_general(six(left, False), six(u, True), TALL, preferred_element_type=F32)
    aug[f : f + 128, f : f + 384] = aug[f : f + 128, f : f + 384] - update


def factor_start(aug, inner):
    aug[:, 0:256] = inner
    r = lax.broadcasted_iota(jnp.int32, (256, 256), 0)
    c = lax.broadcasted_iota(jnp.int32, (256, 256), 1)
    aug[:, 256:512] = jnp.where(r == c, 1.0, 0.0).astype(F32)


def factor_part(aug, first, count):
    @pl.loop(first % 8, first % 8 + count)
    def _(g):
        factor_pair(aug, first // 8, g)

    if first + count == 8:
        aug[128:256, 128:384] = aug[128:256, 128:384] - exact(aug[0:128, 128:256], aug[0:128, 128:384], ((0,), (0,)))


def symmetric(high, low):
    tall = (((0,), (0,)), ((), ()))
    first = lax.dot_general(high, jnp.concatenate([high, low], axis=1), tall, preferred_element_type=F32)
    last = lax.dot_general(low, low, tall, preferred_element_type=F32)
    return first, last


def kernel(sizes, start, x_hbm, basis, scaled, x, xt, gath, y, part, sum1, got1, got2, aug,
           mine, mgot1, mgot2, mgot3, mall, tbuf, xsem, gs, gr, hs, hr, ls, lr, ks, kr, ms, mr, ts, tr):
    blk = lax.axis_index("blk")
    smp = lax.axis_index("smp")
    at = [smp // 16, lax.rem(smp // 4, 4), lax.rem(smp, 4)]

    def peer(axis, pos):
        where = list(at)
        where[axis] = pos
        return (blk, where[0] * 16 + where[1] * 4 + where[2])

    load = pltpu.make_async_copy(x_hbm, x, xsem)
    load.start()
    barrier = pltpu.get_barrier_semaphore()
    steps = [(dz, dy, dx) for dz in range(4) for dy in range(4) for dx in range(4) if 0 < (dz > 0) + (dy > 0) + (dx > 0) < 3]
    for step in steps:
        z, y_, x_ = (lax.rem(p + d, 4) for p, d in zip(at, step))
        pl.semaphore_signal(barrier, inc=1, device_id=(blk, z * 16 + y_ * 4 + x_), device_id_type=MESH)
    pl.semaphore_signal(barrier, inc=1, device_id=(1 - blk, smp), device_id_type=MESH)

    size = sizes[0]
    live = lax.broadcasted_iota(jnp.int32, (32, 256), 0) + smp * 32 < size

    def put_own(buf, rows):
        high = rows.astype(BF16)
        low = (rows - high.astype(F32)).astype(BF16)
        for i, v in enumerate((high[:, :128], high[:, 128:], low[:, :128], low[:, 128:])):
            buf[at[0], at[1], at[2], 32 * i : 32 * i + 32, :] = v

    put_own(gath.at[0], jnp.where(live, start[0], 0.0))
    pl.semaphore_wait(barrier, len(steps) + 1)

    def copies(src, dst, send, recv, axis, ds=(1, 2, 3)):
        for d in ds:
            pos = lax.rem(at[axis] + d, 4)
            pltpu.make_async_remote_copy(
                src_ref=src(pos), dst_ref=dst(d), send_sem=send, recv_sem=recv,
                device_id=peer(axis, pos), device_id_type=MESH,
            ).start()

    def drain(sem, like):
        pltpu.make_async_copy(like, like, sem).wait()

    def pick(axis_index, n, pos):
        return tuple(pos if i == axis_index else slice(None) for i in range(n))

    def place(c, pc, pu, rest=()):
        idx = [slice(None)] * 3
        idx[c], idx[OTHERS[c][0]] = pc, pu
        return tuple(idx) + rest

    def plane_copy(c, du, dv, src, dst, send, recv):
        u, v = OTHERS[c]
        where = list(at)
        where[u] = lax.rem(at[u] + du, 4)
        where[v] = lax.rem(at[v] + dv, 4)
        pltpu.make_async_remote_copy(
            src_ref=src, dst_ref=dst, send_sem=send, recv_sem=recv,
            device_id=(blk, where[0] * 16 + where[1] * 4 + where[2]), device_id_type=MESH,
        ).start()

    def gather(phase):
        buf = gath.at[phase % 2]
        for du in (0, 1, 3, 2):
            for c in range(3):
                view = buf.at[at[0], at[1], at[2], pl.ds(*GATHER_ROWS[c])]
                for dv in range(4):
                    if du + dv:
                        plane_copy(c, du, dv, view, view, gs.at[c, min(du, 1)], gr.at[c, du])
        yield
        for du in (0, 1, 3, 2):
            for c in range(3):
                rows = pl.ds(*GATHER_ROWS[c])
                drain(gr.at[c, du], buf.at[0, 0, 0 : 4 if du else 3, rows])
                line = lax.rem(at[OTHERS[c][0]] + 4 - du, 4)
                view = buf.at[place(c, at[c], line, (rows,))]
                copies(lambda pos: view, lambda d: view, hs.at[c], hr.at[c], c)
        for c in range(3):
            rows = pl.ds(*GATHER_ROWS[c])
            drain(gs.at[c, 0], buf.at[0, 0, 0:3, rows])
            drain(gs.at[c, 1], buf.at[0, 0:3, :, rows])
            drain(hs.at[c], buf.at[0:3, :, :, rows])
            drain(hr.at[c], buf.at[0:3, :, :, rows])

    def halves(buf):
        full = buf[...]
        p = [full[:, :, :, 32 * i : 32 * i + 32, :].reshape(CAP, 128) for i in range(4)]
        return jnp.concatenate(p[:2], axis=1), jnp.concatenate(p[2:], axis=1)

    def project(phase):
        @pl.loop(0, 2)
        def _(m):
            rows = pl.ds(pl.multiple_of(m * 512, 512), 512)
            high, low = halves(gath.at[phase])
            t = jnp.dot(x[rows, :], high, preferred_element_type=F32) + jnp.dot(x[rows, :], low, preferred_element_type=F32)
            th = t.astype(BF16)
            y[rows, 0:256] = th
            y[rows, 256:512] = (t - th.astype(F32)).astype(BF16)

    def expand(z):
        @pl.loop(0, 2)
        def _(m):
            rows = pl.ds(pl.multiple_of(z * 512 + m * 256, 256), 256)
            t = jnp.dot(xt[rows, :], y[:, 0:256], preferred_element_type=F32)
            t = t + jnp.dot(xt[rows, :], y[:, 256:512], preferred_element_type=F32)
            part[z, pl.ds(2 * m, 2), :, 0:32, :] = t[:, :128].reshape(2, 4, 32, 128)
            part[z, pl.ds(2 * m, 2), :, 32:64, :] = t[:, 128:].reshape(2, 4, 32, 128)

    def scatter(phase, result):
        def send(c, du, d):
            rows = (pl.ds(*SUM_ROWS[c]),)
            line = lax.rem(at[OTHERS[c][0]] + du, 4)
            copies(
                lambda pos: part.at[place(c, pos, line, rows)], lambda d: got1.at[(d - 1, du, slice(None)) + rows],
                ls.at[c], lr.at[c, du], c, d)

        for du in (2, 1, 3, 0):
            expand(lax.rem(at[0] + du, 4))
            for c in (1, 2):
                send(c, du, (1, 2, 3))
            if du:
                for line in (2, 1, 3, 0):
                    send(0, line, (du,))
        yield
        for du in (2, 1, 3, 0):
            for c in range(3):
                r0, n = SUM_ROWS[c]
                drain(lr.at[c, du], got1.at[:, du, :, pl.ds(r0, n)])
                line = lax.rem(at[OTHERS[c][0]] + du, 4)
                v = part[place(c, at[c], line, (slice(r0, r0 + n),))]
                for d in range(3):
                    v = v + got1[d, du, :, r0 : r0 + n, :]
                sum1[du, :, r0 : r0 + n, :] = v
                for dv in range(4):
                    if du + dv:
                        pv = lax.rem(at[OTHERS[c][1]] + dv, 4)
                        plane_copy(
                            c, du, dv, sum1.at[du, pv, pl.ds(r0, n)], got2.at[4 * du + dv - 1, pl.ds(r0, n)],
                            ks.at[c], kr.at[c])
            yield
        pieces = []
        for c in range(3):
            r0, n = SUM_ROWS[c]
            drain(ls.at[c], got1.at[:, :, :, pl.ds(r0, n)])
            drain(ks.at[c], got2.at[:, pl.ds(r0, n)])
            drain(kr.at[c], got2.at[:, pl.ds(r0, n)])
            v = sum1[0, at[OTHERS[c][1]], r0 : r0 + n, :]
            for i in range(15):
                v = v + got2[i, r0 : r0 + n, :]
            pieces.append(v)
        v = jnp.concatenate(pieces, axis=0)
        v = jnp.concatenate([v[:32], v[32:]], axis=1)
        result.append(jnp.where(live, v * (1.0 / (64 * 1024)), 0.0))

    def square(phase):
        high, low = halves(gath.at[phase])
        first, last = symmetric(high, low)
        cross = first[:, 256:512]
        return first[:, 0:256] + (cross + cross.T) + last

    def run(gen):
        for _ in gen:
            pass

    g = gather(0)
    next(g)
    load.wait()

    @pl.loop(0, 8)
    def _(m):
        cols = pl.ds(pl.multiple_of(m * 256, 256), 256)
        xt[cols, :] = x[:, cols].T

    run(g)
    project(0)
    out = []
    run(scatter(0, out))
    put_own(gath.at[1], out[0])
    run(gather(1))
    project(1)
    out = []
    s = scatter(1, out)
    next(s)
    factor_start(aug, square(1))
    factor_part(aug, 0, 4)
    next(s)
    factor_part(aug, 4, 2)
    next(s)
    factor_part(aug, 6, 2)
    next(s)
    factor_part(aug, 8, 2)
    next(s)
    factor_part(aug, 10, 6)
    run(s)
    image = exact(out[0], aug[:, 256:512], ((1,), (1,)))
    put_own(gath.at[0], image)
    run(gather(2))
    project(0)

    first, last = symmetric(y[:, 0:256], y[:, 256:512])
    cross = first[:, 256:512]
    total = (first[:, 0:256] + (cross + cross.T) + last) * (1.0 / (64 * 1024))
    for c, (r, q) in enumerate(((0, 0), (0, 128), (128, 128))):
        mine[c] = total[r : r + 128, q : q + 128].reshape(4, 32, 128)
    for c, o in enumerate(ORDERS):
        copies(lambda pos: mine.at[c, pos], lambda d: mgot1.at[c, d - 1], ms.at[c, 0], mr.at[c, 0], o[0])
    factor_start(aug, square(0))
    factor_part(aug, 0, 4)
    for stage, (had, now) in ((1, (None, mgot2)), (2, (mgot2, mgot3)), (3, (mgot3, mall))):
        for c, o in enumerate(ORDERS):
            drain(mr.at[c, stage - 1], mgot1.at[c])
            drain(ms.at[c, stage - 1], mgot1.at[c])
            if stage == 1:
                v = mine[c, at[o[0]]] + mgot1[c, 0] + mgot1[c, 1] + mgot1[c, 2]
            else:
                v = had[c, 0] + had[c, 1] + had[c, 2] + had[c, 3]
            axis = o[stage] if stage < 3 else o[0]
            now[c, at[axis]] = v
            view = now.at[c, at[axis]]
            copies(lambda pos: view, lambda d: view, ms.at[c, stage], mr.at[c, stage], axis)
        factor_part(aug, 4 * stage, 4)
    low = aug[:, 256:512]
    basis[0] = exact(image, low, ((1,), (1,))) * math.sqrt(CAP)
    for c in range(3):
        drain(mr.at[c, 3], mgot1.at[c])
        drain(ms.at[c, 3], mgot1.at[c])
    b00, b01, b11 = (mall[c].reshape(128, 128) for c in range(3))
    full = jnp.concatenate([jnp.concatenate([b00, b01], axis=1), jnp.concatenate([b01.T, b11], axis=1)], axis=0)
    left = exact(low, full, ((1,), (0,)))
    tbuf[0] = jnp.broadcast_to(jnp.sum(left * low, axis=(0, 1), keepdims=True), (8, 128))
    c = pltpu.make_async_remote_copy(
        src_ref=tbuf.at[0], dst_ref=tbuf.at[1], send_sem=ts, recv_sem=tr, device_id=(1 - blk, smp), device_id_type=MESH
    )
    c.start()
    ray = exact(left, low, ((1,), (1,)))
    c.wait()
    both = tbuf[0, 0:1, 0:1] + tbuf[1, 0:1, 0:1]
    scaled[0] = ray * (2.0 * K) / both


def hand_out(basis, scaled, basis_out, scaled_out):
    basis_out[...] = basis[...]
    scaled_out[...] = scaled[...]


def body(genotypes, sizes, start):
    vm = pltpu.VMEM
    dma = pltpu.SemaphoreType.DMA
    shapes = (jax.ShapeDtypeStruct((1, 32, K), F32), jax.ShapeDtypeStruct((1, K, K), F32))
    results = pl.pallas_call(
        kernel,
        out_shape=shapes,
        in_specs=[
            pl.BlockSpec(memory_space=pltpu.SMEM),
            pl.BlockSpec(memory_space=pltpu.VMEM),
            pl.BlockSpec(memory_space=pl.ANY),
        ],
        out_specs=(pl.BlockSpec(memory_space=pltpu.VMEM), pl.BlockSpec(memory_space=pltpu.VMEM)),
        scratch_shapes=[
            vm((1024, CAP), BF16),
            vm((CAP, 1024), BF16),
            vm((2, 4, 4, 4, 128, 128), BF16),
            vm((1024, 512), BF16),
            vm((4, 4, 4, 64, 128), F32),
            vm((4, 4, 64, 128), F32),
            vm((3, 4, 4, 64, 128), F32),
            vm((15, 64, 128), F32),
            vm((K, 2 * K), F32),
            vm((3, 4, 32, 128), F32),
            vm((3, 3, 32, 128), F32),
            vm((3, 4, 32, 128), F32),
            vm((3, 4, 32, 128), F32),
            vm((3, 4, 32, 128), F32),
            vm((2, 8, 128), F32),
            dma,
            dma((3, 2)),
            dma((3, 4)),
            dma((3,)),
            dma((3,)),
            dma((3,)),
            dma((3, 4)),
            dma((3,)),
            dma((3,)),
            dma((3, 4)),
            dma((3, 4)),
            dma,
            dma,
        ],
        compiler_params=pltpu.CompilerParams(
            collective_id=0, has_side_effects=True, vmem_limit_bytes=60 * 2**20
        ),
    )(sizes, start, genotypes.reshape(genotypes.shape[1:]))
    return pl.pallas_call(hand_out, out_shape=shapes)(*results)


def solution(mesh):
    return jax.shard_map(
        body,
        mesh=mesh,
        in_specs=(P("blk", "smp", None), P("blk"), P("blk", "smp", None)),
        out_specs=(P("blk", "smp", None), P("blk", None, None)),
        check_vma=False,
    )
```

```python
import functools
import math

import jax
import jax.numpy as jnp
from jax import lax
from jax.experimental import pallas as pl
from jax.experimental.pallas import tpu as pltpu
from jax.sharding import PartitionSpec as P

CAP = 2048
K = 256
F32 = jnp.float32
BF16 = jnp.bfloat16
MESH = pl.DeviceIdType.MESH
OTHERS = ((1, 2), (0, 2), (0, 1))
ORDERS = ((0, 1, 2), (1, 2, 0), (2, 0, 1))
SUM_ROWS = ((0, 24), (24, 24), (48, 16))
GATHER_ROWS = ((0, 48), (48, 48), (96, 32))


def split3(v):
    high = v.astype(BF16).astype(F32)
    rest = v - high
    middle = rest.astype(BF16).astype(F32)
    return high, middle, rest - middle


def exact(a, b, dims):
    return lax.dot_general(
        a, b, (dims, ((), ())), precision=lax.Precision.HIGHEST, preferred_element_type=F32
    )


def spread(block, first):
    return [jnp.broadcast_to(block[:, first + s : first + s + 1], (8, 128)) for s in range(8)]


def row_of(v, t):
    return jnp.broadcast_to(v[t : t + 1, :], v.shape)


def total(terms):
    terms = list(terms)
    while len(terms) > 1:
        terms = [terms[i] + terms[i + 1] if i + 1 < len(terms) else terms[i] for i in range(0, len(terms), 2)]
    return terms[0]


def factor8(columns):
    a = {(t, s): row_of(columns[s], t) for s in range(8) for t in range(s, 8)}
    inv = []
    for s in range(8):
        r = lax.rsqrt(a[s, s])
        inv.append(r)
        for t in range(s + 1, 8):
            a[t, s] = a[t, s] * r
        for t in range(s + 1, 8):
            for u in range(s + 1, t + 1):
                a[t, u] = a[t, u] - a[t, s] * a[u, s]
    w = {}
    for s in range(8):
        w[s, s] = inv[s]
        for t in range(s + 1, 8):
            acc = a[t, s] * w[s, s]
            for u in range(s + 1, t):
                acc = acc + a[t, u] * w[u, s]
            w[t, s] = -acc * inv[t]
    return w


def stack_rows(w):
    sub = lax.broadcasted_iota(jnp.int32, (8, 128), 0)
    columns = []
    for s in range(8):
        col = jnp.where(sub == s, w[s, s], 0.0)
        for t in range(s + 1, 8):
            col = jnp.where(sub == t, w[t, s], col)
        columns.append(wide(col))
    return columns


def wide(col):
    return jnp.concatenate([col] * 3, axis=1)


def six(v, right):
    a, b, c = split3(v)
    return jnp.concatenate([a, b, a, b, c, a] if right else [a, a, b, b, a, c], axis=0).astype(BF16)


TALL = (((0,), (0,)), ((), ()))


def factor_pair(aug, half, g):
    f = half * 128
    row = pl.multiple_of(f + g * 16, 16)
    next_row = pl.multiple_of(row + 8, 8)
    p1 = aug[pl.ds(row, 8), f : f + 384]
    p2 = aug[pl.ds(next_row, 8), f : f + 384]
    shift = lax.rem(128 - g * 16, 128)
    b1 = pltpu.roll(p1[:, 0:128], shift, 1)
    b2 = pltpu.roll(p2[:, 0:128], shift, 1)
    w1 = factor8(spread(b1, 0))
    cross = spread(b2, 0)
    low = [total(cross[k] * w1[s, k] for k in range(s + 1)) for s in range(8)]
    back = [total(low[s] * w1[s, k] for s in range(k, 8)) for k in range(8)]
    b2 = b2 - total(back[k] * row_of(b1, k) for k in range(8))
    w2 = factor8(spread(b2, 8))
    c1 = stack_rows(w1)
    rows1 = [row_of(p1, k) for k in range(8)]
    u1 = total(c1[k] * rows1[k] for k in range(8))
    p2 = p2 - total(wide(back[k]) * rows1[k] for k in range(8))
    c2 = stack_rows(w2)
    u2 = total(c2[k] * row_of(p2, k) for k in range(8))
    aug[pl.ds(row, 8), f : f + 384] = u1
    aug[pl.ds(next_row, 8), f : f + 384] = u2
    u = jnp.concatenate([u1, u2], axis=0)
    left = u[:, 0:128]
    lane = lax.broadcasted_iota(jnp.int32, left.shape, 1)
    left = jnp.where(lane > g * 16 + 15, left, 0.0)
    update = lax.dot_general(six(left, False), six(u, True), TALL, preferred_element_type=F32)
    aug[f : f + 128, f : f + 384] = aug[f : f + 128, f : f + 384] - update


def factor_start(aug, inner):
    aug[:, 0:256] = inner
    r = lax.broadcasted_iota(jnp.int32, (256, 256), 0)
    c = lax.broadcasted_iota(jnp.int32, (256, 256), 1)
    aug[:, 256:512] = jnp.where(r == c, 1.0, 0.0).astype(F32)


def factor_part(aug, first, count):
    @pl.loop(first % 8, first % 8 + count)
    def _(g):
        factor_pair(aug, first // 8, g)

    if first + count == 8:
        aug[128:256, 128:384] = aug[128:256, 128:384] - exact(aug[0:128, 128:256], aug[0:128, 128:384], ((0,), (0,)))


def symmetric(high, low):
    tall = (((0,), (0,)), ((), ()))
    first = lax.dot_general(high, jnp.concatenate([high, low], axis=1), tall, preferred_element_type=F32)
    last = lax.dot_general(low, low, tall, preferred_element_type=F32)
    return first, last


def kernel(sizes_hbm, start_hbm, x_hbm, basis, scaled, x, xt, gath, y, part, sum1, got1, got2, aug,
           mine, mgot1, mgot2, mgot3, mall, tbuf, sizes, start, xsem, isem, gs, gr, hs, hr, ls, lr, ks, kr, ms, mr, ts, tr):
    blk = lax.axis_index("blk")
    smp = lax.axis_index("smp")
    at = [smp // 16, lax.rem(smp // 4, 4), lax.rem(smp, 4)]

    def peer(axis, pos):
        where = list(at)
        where[axis] = pos
        return (blk, where[0] * 16 + where[1] * 4 + where[2])

    small = (pltpu.make_async_copy(sizes_hbm, sizes, isem.at[0]), pltpu.make_async_copy(start_hbm, start, isem.at[1]))
    load = pltpu.make_async_copy(x_hbm, x, xsem)
    for copy in small:
        copy.start()
    barrier = pltpu.get_barrier_semaphore()
    steps = [(dz, dy, dx) for dz in range(4) for dy in range(4) for dx in range(4) if 0 < (dz > 0) + (dy > 0) + (dx > 0) < 3]
    for step in steps:
        z, y_, x_ = (lax.rem(p + d, 4) for p, d in zip(at, step))
        pl.semaphore_signal(barrier, inc=1, device_id=(blk, z * 16 + y_ * 4 + x_), device_id_type=MESH)
    pl.semaphore_signal(barrier, inc=1, device_id=(1 - blk, smp), device_id_type=MESH)

    load.start()
    for copy in small:
        copy.wait()
    size = sizes[0]
    live = lax.broadcasted_iota(jnp.int32, (32, 256), 0) + smp * 32 < size

    def put_own(buf, rows):
        high = rows.astype(BF16)
        low = (rows - high.astype(F32)).astype(BF16)
        for i, v in enumerate((high[:, :128], high[:, 128:], low[:, :128], low[:, 128:])):
            buf[at[0], at[1], at[2], 32 * i : 32 * i + 32, :] = v

    put_own(gath.at[0], jnp.where(live, start[0], 0.0))
    pl.semaphore_wait(barrier, len(steps) + 1)

    def copies(src, dst, send, recv, axis, ds=(1, 2, 3)):
        for d in ds:
            pos = lax.rem(at[axis] + d, 4)
            pltpu.make_async_remote_copy(
                src_ref=src(pos), dst_ref=dst(d), send_sem=send, recv_sem=recv,
                device_id=peer(axis, pos), device_id_type=MESH,
            ).start()

    def drain(sem, like):
        pltpu.make_async_copy(like, like, sem).wait()

    def pick(axis_index, n, pos):
        return tuple(pos if i == axis_index else slice(None) for i in range(n))

    def place(c, pc, pu, rest=()):
        idx = [slice(None)] * 3
        idx[c], idx[OTHERS[c][0]] = pc, pu
        return tuple(idx) + rest

    def plane_copy(c, du, dv, src, dst, send, recv):
        u, v = OTHERS[c]
        where = list(at)
        where[u] = lax.rem(at[u] + du, 4)
        where[v] = lax.rem(at[v] + dv, 4)
        pltpu.make_async_remote_copy(
            src_ref=src, dst_ref=dst, send_sem=send, recv_sem=recv,
            device_id=(blk, where[0] * 16 + where[1] * 4 + where[2]), device_id_type=MESH,
        ).start()

    def gather(phase):
        buf = gath.at[phase % 2]
        for du in (0, 1, 3, 2):
            for c in range(3):
                view = buf.at[at[0], at[1], at[2], pl.ds(*GATHER_ROWS[c])]
                for dv in range(4):
                    if du + dv:
                        plane_copy(c, du, dv, view, view, gs.at[c, min(du, 1)], gr.at[c, du])
        yield
        for du in (0, 1, 3, 2):
            for c in range(3):
                rows = pl.ds(*GATHER_ROWS[c])
                drain(gr.at[c, du], buf.at[0, 0, 0 : 4 if du else 3, rows])
                line = lax.rem(at[OTHERS[c][0]] + 4 - du, 4)
                view = buf.at[place(c, at[c], line, (rows,))]
                copies(lambda pos: view, lambda d: view, hs.at[c], hr.at[c], c)
        for c in range(3):
            rows = pl.ds(*GATHER_ROWS[c])
            drain(gs.at[c, 0], buf.at[0, 0, 0:3, rows])
            drain(gs.at[c, 1], buf.at[0, 0:3, :, rows])
            drain(hs.at[c], buf.at[0:3, :, :, rows])
            drain(hr.at[c], buf.at[0:3, :, :, rows])

    def halves(buf):
        full = buf[...]
        p = [full[:, :, :, 32 * i : 32 * i + 32, :].reshape(CAP, 128) for i in range(4)]
        return jnp.concatenate(p[:2], axis=1), jnp.concatenate(p[2:], axis=1)

    def project(phase):
        @pl.loop(0, 2)
        def _(m):
            rows = pl.ds(pl.multiple_of(m * 512, 512), 512)
            high, low = halves(gath.at[phase])
            t = jnp.dot(x[rows, :], high, preferred_element_type=F32) + jnp.dot(x[rows, :], low, preferred_element_type=F32)
            th = t.astype(BF16)
            y[rows, 0:256] = th
            y[rows, 256:512] = (t - th.astype(F32)).astype(BF16)

    def expand(z):
        @pl.loop(0, 2)
        def _(m):
            rows = pl.ds(pl.multiple_of(z * 512 + m * 256, 256), 256)
            t = jnp.dot(xt[rows, :], y[:, 0:256], preferred_element_type=F32)
            t = t + jnp.dot(xt[rows, :], y[:, 256:512], preferred_element_type=F32)
            part[z, pl.ds(2 * m, 2), :, 0:32, :] = t[:, :128].reshape(2, 4, 32, 128)
            part[z, pl.ds(2 * m, 2), :, 32:64, :] = t[:, 128:].reshape(2, 4, 32, 128)

    def scatter(phase, result):
        def send(c, du, d):
            rows = (pl.ds(*SUM_ROWS[c]),)
            line = lax.rem(at[OTHERS[c][0]] + du, 4)
            copies(
                lambda pos: part.at[place(c, pos, line, rows)], lambda d: got1.at[(d - 1, du, slice(None)) + rows],
                ls.at[c], lr.at[c, du], c, d)

        for du in (2, 1, 3, 0):
            expand(lax.rem(at[0] + du, 4))
            for c in (1, 2):
                send(c, du, (1, 2, 3))
            if du:
                for line in (2, 1, 3, 0):
                    send(0, line, (du,))
        yield
        for du in (2, 1, 3, 0):
            for c in range(3):
                r0, n = SUM_ROWS[c]
                drain(lr.at[c, du], got1.at[:, du, :, pl.ds(r0, n)])
                line = lax.rem(at[OTHERS[c][0]] + du, 4)
                v = part[place(c, at[c], line, (slice(r0, r0 + n),))]
                for d in range(3):
                    v = v + got1[d, du, :, r0 : r0 + n, :]
                sum1[du, :, r0 : r0 + n, :] = v
                for dv in range(4):
                    if du + dv:
                        pv = lax.rem(at[OTHERS[c][1]] + dv, 4)
                        plane_copy(
                            c, du, dv, sum1.at[du, pv, pl.ds(r0, n)], got2.at[4 * du + dv - 1, pl.ds(r0, n)],
                            ks.at[c], kr.at[c])
            yield
        pieces = []
        for c in range(3):
            r0, n = SUM_ROWS[c]
            drain(ls.at[c], got1.at[:, :, :, pl.ds(r0, n)])
            drain(ks.at[c], got2.at[:, pl.ds(r0, n)])
            drain(kr.at[c], got2.at[:, pl.ds(r0, n)])
            v = sum1[0, at[OTHERS[c][1]], r0 : r0 + n, :]
            for i in range(15):
                v = v + got2[i, r0 : r0 + n, :]
            pieces.append(v)
        v = jnp.concatenate(pieces, axis=0)
        v = jnp.concatenate([v[:32], v[32:]], axis=1)
        result.append(jnp.where(live, v * (1.0 / (64 * 1024)), 0.0))

    def square(phase):
        high, low = halves(gath.at[phase])
        first, last = symmetric(high, low)
        cross = first[:, 256:512]
        return first[:, 0:256] + (cross + cross.T) + last

    def run(gen):
        for _ in gen:
            pass

    g = gather(0)
    next(g)
    load.wait()

    @pl.loop(0, 8)
    def _(m):
        cols = pl.ds(pl.multiple_of(m * 256, 256), 256)
        xt[cols, :] = x[:, cols].T

    run(g)
    project(0)
    out = []
    run(scatter(0, out))
    put_own(gath.at[1], out[0])
    run(gather(1))
    project(1)
    out = []
    s = scatter(1, out)
    next(s)
    factor_start(aug, square(1))
    for first, count in ((0, 5), (5, 1), (6, 2), (8, 3), (11, 5)):
        factor_part(aug, first, count)
        next(s, None)
    image = exact(out[0], aug[:, 256:512], ((1,), (1,)))
    put_own(gath.at[0], image)
    run(gather(2))
    project(0)

    first, last = symmetric(y[:, 0:256], y[:, 256:512])
    cross = first[:, 256:512]
    total = (first[:, 0:256] + (cross + cross.T) + last) * (1.0 / (64 * 1024))
    for c, (r, q) in enumerate(((0, 0), (0, 128), (128, 128))):
        mine[c] = total[r : r + 128, q : q + 128].reshape(4, 32, 128)
    for c, o in enumerate(ORDERS):
        copies(lambda pos: mine.at[c, pos], lambda d: mgot1.at[c, d - 1], ms.at[c, 0], mr.at[c, 0], o[0])
    factor_start(aug, square(0))
    factor_part(aug, 0, 3)
    for stage, had, now, pairs in ((1, None, mgot2, (3, 5)), (2, mgot2, mgot3, (8, 5)), (3, mgot3, mall, (13, 3))):
        for c, o in enumerate(ORDERS):
            drain(mr.at[c, stage - 1], mgot1.at[c])
            drain(ms.at[c, stage - 1], mgot1.at[c])
            if stage == 1:
                v = mine[c, at[o[0]]] + mgot1[c, 0] + mgot1[c, 1] + mgot1[c, 2]
            else:
                v = had[c, 0] + had[c, 1] + had[c, 2] + had[c, 3]
            axis = o[stage] if stage < 3 else o[0]
            now[c, at[axis]] = v
            view = now.at[c, at[axis]]
            copies(lambda pos: view, lambda d: view, ms.at[c, stage], mr.at[c, stage], axis)
        factor_part(aug, *pairs)
    low = aug[:, 256:512]
    for c in range(3):
        drain(mr.at[c, 3], mgot1.at[c])
        drain(ms.at[c, 3], mgot1.at[c])
    b00, b01, b11 = (mall[c].reshape(128, 128) for c in range(3))
    full = jnp.concatenate([jnp.concatenate([b00, b01], axis=1), jnp.concatenate([b01.T, b11], axis=1)], axis=0)
    left = exact(low, full, ((1,), (0,)))
    tbuf[0] = jnp.broadcast_to(jnp.sum(left * low, axis=(0, 1), keepdims=True), (8, 128))
    c = pltpu.make_async_remote_copy(
        src_ref=tbuf.at[0], dst_ref=tbuf.at[1], send_sem=ts, recv_sem=tr, device_id=(1 - blk, smp), device_id_type=MESH
    )
    c.start()
    ray = exact(left, low, ((1,), (1,)))
    basis[0] = exact(image, low, ((1,), (1,))) * math.sqrt(CAP)
    c.wait()
    both = tbuf[0, 0:1, 0:1] + tbuf[1, 0:1, 0:1]
    scaled[0] = ray * (2.0 * K) / both


def hand_out(basis, scaled, basis_out, scaled_out):
    basis_out[...] = basis[...]
    scaled_out[...] = scaled[...]


def body(genotypes, sizes, start):
    vm = pltpu.VMEM
    dma = pltpu.SemaphoreType.DMA
    shapes = (jax.ShapeDtypeStruct((1, 32, K), F32), jax.ShapeDtypeStruct((1, K, K), F32))
    results = pl.pallas_call(
        kernel,
        out_shape=shapes,
        in_specs=[
            pl.BlockSpec(memory_space=pl.ANY),
            pl.BlockSpec(memory_space=pl.ANY),
            pl.BlockSpec(memory_space=pl.ANY),
        ],
        out_specs=(pl.BlockSpec(memory_space=pltpu.VMEM), pl.BlockSpec(memory_space=pltpu.VMEM)),
        scratch_shapes=[
            vm((1024, CAP), BF16),
            vm((CAP, 1024), BF16),
            vm((2, 4, 4, 4, 128, 128), BF16),
            vm((1024, 512), BF16),
            vm((4, 4, 4, 64, 128), F32),
            vm((4, 4, 64, 128), F32),
            vm((3, 4, 4, 64, 128), F32),
            vm((15, 64, 128), F32),
            vm((K, 2 * K), F32),
            vm((3, 4, 32, 128), F32),
            vm((3, 3, 32, 128), F32),
            vm((3, 4, 32, 128), F32),
            vm((3, 4, 32, 128), F32),
            vm((3, 4, 32, 128), F32),
            vm((2, 8, 128), F32),
            pltpu.SMEM((1,), jnp.int32),
            vm((1, 32, K), F32),
            dma,
            dma((2,)),
            dma((3, 2)),
            dma((3, 4)),
            dma((3,)),
            dma((3,)),
            dma((3,)),
            dma((3, 4)),
            dma((3,)),
            dma((3,)),
            dma((3, 4)),
            dma((3, 4)),
            dma,
            dma,
        ],
        compiler_params=pltpu.CompilerParams(
            collective_id=0, has_side_effects=True, vmem_limit_bytes=60 * 2**20
        ),
    )(sizes, start, genotypes.reshape(genotypes.shape[1:]))
    return pl.pallas_call(hand_out, out_shape=shapes)(*results)


def solution(mesh):
    return jax.shard_map(
        body,
        mesh=mesh,
        in_specs=(P("blk", "smp", None), P("blk"), P("blk", "smp", None)),
        out_specs=(P("blk", "smp", None), P("blk", None, None)),
        check_vma=False,
    )
```

```python
import functools
import math

import jax
import jax.numpy as jnp
from jax import lax
from jax.experimental import pallas as pl
from jax.experimental.pallas import tpu as pltpu
from jax.sharding import PartitionSpec as P

CAP = 2048
K = 256
F32 = jnp.float32
BF16 = jnp.bfloat16
MESH = pl.DeviceIdType.MESH
OTHERS = ((1, 2), (0, 2), (0, 1))
ORDERS = ((0, 1, 2), (1, 2, 0), (2, 0, 1))
SUM_ROWS = ((0, 16), (16, 24), (40, 24))
GATHER_ROWS = ((0, 32), (32, 48), (80, 48))


def split3(v):
    high = v.astype(BF16).astype(F32)
    rest = v - high
    middle = rest.astype(BF16).astype(F32)
    return high, middle, rest - middle


def exact(a, b, dims):
    return lax.dot_general(
        a, b, (dims, ((), ())), precision=lax.Precision.HIGHEST, preferred_element_type=F32
    )


def spread(block, first):
    return [jnp.broadcast_to(block[:, first + s : first + s + 1], (8, 128)) for s in range(8)]


def row_of(v, t):
    return jnp.broadcast_to(v[t : t + 1, :], v.shape)


def total(terms):
    terms = list(terms)
    while len(terms) > 1:
        terms = [terms[i] + terms[i + 1] if i + 1 < len(terms) else terms[i] for i in range(0, len(terms), 2)]
    return terms[0]


def factor8(columns):
    a = {(t, s): row_of(columns[s], t) for s in range(8) for t in range(s, 8)}
    inv = []
    for s in range(8):
        r = lax.rsqrt(a[s, s])
        inv.append(r)
        for t in range(s + 1, 8):
            a[t, s] = a[t, s] * r
        for t in range(s + 1, 8):
            for u in range(s + 1, t + 1):
                a[t, u] = a[t, u] - a[t, s] * a[u, s]
    w = {}
    for s in range(8):
        w[s, s] = inv[s]
        for t in range(s + 1, 8):
            acc = a[t, s] * w[s, s]
            for u in range(s + 1, t):
                acc = acc + a[t, u] * w[u, s]
            w[t, s] = -acc * inv[t]
    return w


def stack_rows(w):
    sub = lax.broadcasted_iota(jnp.int32, (8, 128), 0)
    columns = []
    for s in range(8):
        col = jnp.where(sub == s, w[s, s], 0.0)
        for t in range(s + 1, 8):
            col = jnp.where(sub == t, w[t, s], col)
        columns.append(wide(col))
    return columns


def wide(col):
    return jnp.concatenate([col] * 3, axis=1)


def six(v, right):
    a, b, c = split3(v)
    return jnp.concatenate([a, b, a, b, c, a] if right else [a, a, b, b, a, c], axis=0).astype(BF16)


TALL = (((0,), (0,)), ((), ()))


def factor_pair(aug, half, g):
    f = half * 128
    row = pl.multiple_of(f + g * 16, 16)
    next_row = pl.multiple_of(row + 8, 8)
    p1 = aug[pl.ds(row, 8), f : f + 384]
    p2 = aug[pl.ds(next_row, 8), f : f + 384]
    shift = lax.rem(128 - g * 16, 128)
    b1 = pltpu.roll(p1[:, 0:128], shift, 1)
    b2 = pltpu.roll(p2[:, 0:128], shift, 1)
    w1 = factor8(spread(b1, 0))
    cross = spread(b2, 0)
    low = [total(cross[k] * w1[s, k] for k in range(s + 1)) for s in range(8)]
    back = [total(low[s] * w1[s, k] for s in range(k, 8)) for k in range(8)]
    b2 = b2 - total(back[k] * row_of(b1, k) for k in range(8))
    w2 = factor8(spread(b2, 8))
    c1 = stack_rows(w1)
    rows1 = [row_of(p1, k) for k in range(8)]
    u1 = total(c1[k] * rows1[k] for k in range(8))
    p2 = p2 - total(wide(back[k]) * rows1[k] for k in range(8))
    c2 = stack_rows(w2)
    u2 = total(c2[k] * row_of(p2, k) for k in range(8))
    aug[pl.ds(row, 8), f : f + 384] = u1
    aug[pl.ds(next_row, 8), f : f + 384] = u2
    u = jnp.concatenate([u1, u2], axis=0)
    left = u[:, 0:128]
    lane = lax.broadcasted_iota(jnp.int32, left.shape, 1)
    left = jnp.where(lane > g * 16 + 15, left, 0.0)
    update = lax.dot_general(six(left, False), six(u, True), TALL, preferred_element_type=F32)
    aug[f : f + 128, f : f + 384] = aug[f : f + 128, f : f + 384] - update


def factor_start(aug, inner):
    aug[:, 0:256] = inner
    r = lax.broadcasted_iota(jnp.int32, (256, 256), 0)
    c = lax.broadcasted_iota(jnp.int32, (256, 256), 1)
    aug[:, 256:512] = jnp.where(r == c, 1.0, 0.0).astype(F32)


def factor_part(aug, first, count):
    @pl.loop(first % 8, first % 8 + count)
    def _(g):
        factor_pair(aug, first // 8, g)

    if first + count == 8:
        aug[128:256, 128:384] = aug[128:256, 128:384] - exact(aug[0:128, 128:256], aug[0:128, 128:384], ((0,), (0,)))


def symmetric(high, low):
    tall = (((0,), (0,)), ((), ()))
    first = lax.dot_general(high, jnp.concatenate([high, low], axis=1), tall, preferred_element_type=F32)
    last = lax.dot_general(low, low, tall, preferred_element_type=F32)
    return first, last


def kernel(sizes_hbm, start_hbm, x_hbm, basis, scaled, x, xt, gath, y, part, sum1, got1, got2, aug,
           mine, mgot1, mgot2, mgot3, mall, tbuf, sizes, start, xsem, isem, gs, gr, hs, hr, ls, lr, ks, kr, ms, mr, ts, tr):
    blk = lax.axis_index("blk")
    smp = lax.axis_index("smp")
    at = [smp // 16, lax.rem(smp // 4, 4), lax.rem(smp, 4)]

    def peer(axis, pos):
        where = list(at)
        where[axis] = pos
        return (blk, where[0] * 16 + where[1] * 4 + where[2])

    small = (pltpu.make_async_copy(sizes_hbm, sizes, isem.at[0]), pltpu.make_async_copy(start_hbm, start, isem.at[1]))
    load = pltpu.make_async_copy(x_hbm, x, xsem)
    for copy in small:
        copy.start()
    barrier = pltpu.get_barrier_semaphore()
    steps = [(dz, dy, dx) for dz in range(4) for dy in range(4) for dx in range(4) if 0 < (dz > 0) + (dy > 0) + (dx > 0) < 3]
    for step in steps:
        z, y_, x_ = (lax.rem(p + d, 4) for p, d in zip(at, step))
        pl.semaphore_signal(barrier, inc=1, device_id=(blk, z * 16 + y_ * 4 + x_), device_id_type=MESH)
    pl.semaphore_signal(barrier, inc=1, device_id=(1 - blk, smp), device_id_type=MESH)

    load.start()
    for copy in small:
        copy.wait()
    size = sizes[0]
    live = lax.broadcasted_iota(jnp.int32, (32, 256), 0) + smp * 32 < size

    def put_own(buf, rows):
        high = rows.astype(BF16)
        low = (rows - high.astype(F32)).astype(BF16)
        for i, v in enumerate((high[:, :128], high[:, 128:], low[:, :128], low[:, 128:])):
            buf[at[0], at[1], at[2], 32 * i : 32 * i + 32, :] = v

    put_own(gath.at[0], jnp.where(live, start[0], 0.0))
    pl.semaphore_wait(barrier, len(steps) + 1)

    def copies(src, dst, send, recv, axis, ds=(1, 2, 3)):
        for d in ds:
            pos = lax.rem(at[axis] + d, 4)
            pltpu.make_async_remote_copy(
                src_ref=src(pos), dst_ref=dst(d), send_sem=send, recv_sem=recv,
                device_id=peer(axis, pos), device_id_type=MESH,
            ).start()

    def drain(sem, like):
        pltpu.make_async_copy(like, like, sem).wait()

    def pick(axis_index, n, pos):
        return tuple(pos if i == axis_index else slice(None) for i in range(n))

    def place(c, pc, pu, rest=()):
        idx = [slice(None)] * 3
        idx[c], idx[OTHERS[c][0]] = pc, pu
        return tuple(idx) + rest

    def plane_copy(c, du, dv, src, dst, send, recv):
        u, v = OTHERS[c]
        where = list(at)
        where[u] = lax.rem(at[u] + du, 4)
        where[v] = lax.rem(at[v] + dv, 4)
        pltpu.make_async_remote_copy(
            src_ref=src, dst_ref=dst, send_sem=send, recv_sem=recv,
            device_id=(blk, where[0] * 16 + where[1] * 4 + where[2]), device_id_type=MESH,
        ).start()

    def gather(phase):
        buf = gath.at[phase % 2]
        for du in (0, 1, 3, 2):
            for c in range(3):
                view = buf.at[at[0], at[1], at[2], pl.ds(*GATHER_ROWS[c])]
                for dv in range(4):
                    if du + dv:
                        plane_copy(c, du, dv, view, view, gs.at[c, min(du, 1)], gr.at[c, du])
        yield
        for du in (0, 1, 3, 2):
            for c in range(3):
                rows = pl.ds(*GATHER_ROWS[c])
                drain(gr.at[c, du], buf.at[0, 0, 0 : 4 if du else 3, rows])
                line = lax.rem(at[OTHERS[c][0]] + 4 - du, 4)
                view = buf.at[place(c, at[c], line, (rows,))]
                copies(lambda pos: view, lambda d: view, hs.at[c], hr.at[c], c)
        for c in range(3):
            rows = pl.ds(*GATHER_ROWS[c])
            drain(gs.at[c, 0], buf.at[0, 0, 0:3, rows])
            drain(gs.at[c, 1], buf.at[0, 0:3, :, rows])
            drain(hs.at[c], buf.at[0:3, :, :, rows])
            drain(hr.at[c], buf.at[0:3, :, :, rows])

    def halves(buf):
        full = buf[...]
        p = [full[:, :, :, 32 * i : 32 * i + 32, :].reshape(CAP, 128) for i in range(4)]
        return jnp.concatenate(p[:2], axis=1), jnp.concatenate(p[2:], axis=1)

    def project(phase):
        @pl.loop(0, 2)
        def _(m):
            rows = pl.ds(pl.multiple_of(m * 512, 512), 512)
            high, low = halves(gath.at[phase])
            t = jnp.dot(x[rows, :], high, preferred_element_type=F32) + jnp.dot(x[rows, :], low, preferred_element_type=F32)
            th = t.astype(BF16)
            y[rows, 0:256] = th
            y[rows, 256:512] = (t - th.astype(F32)).astype(BF16)

    def expand(z):
        @pl.loop(0, 2)
        def _(m):
            rows = pl.ds(pl.multiple_of(z * 512 + m * 256, 256), 256)
            t = jnp.dot(xt[rows, :], y[:, 0:256], preferred_element_type=F32)
            t = t + jnp.dot(xt[rows, :], y[:, 256:512], preferred_element_type=F32)
            part[z, pl.ds(2 * m, 2), :, 0:32, :] = t[:, :128].reshape(2, 4, 32, 128)
            part[z, pl.ds(2 * m, 2), :, 32:64, :] = t[:, 128:].reshape(2, 4, 32, 128)

    def scatter(phase, result):
        def send(c, du, d):
            rows = (pl.ds(*SUM_ROWS[c]),)
            line = lax.rem(at[OTHERS[c][0]] + du, 4)
            copies(
                lambda pos: part.at[place(c, pos, line, rows)], lambda d: got1.at[(d - 1, du, slice(None)) + rows],
                ls.at[c], lr.at[c, du], c, d)

        for du in (2, 1, 3, 0):
            expand(lax.rem(at[0] + du, 4))
            for c in (1, 2):
                send(c, du, (1, 2, 3))
            if du:
                for line in (2, 1, 3, 0):
                    send(0, line, (du,))
        yield
        for du in (2, 1, 3, 0):
            for c in range(3):
                r0, n = SUM_ROWS[c]
                drain(lr.at[c, du], got1.at[:, du, :, pl.ds(r0, n)])
                line = lax.rem(at[OTHERS[c][0]] + du, 4)
                v = part[place(c, at[c], line, (slice(r0, r0 + n),))]
                for d in range(3):
                    v = v + got1[d, du, :, r0 : r0 + n, :]
                sum1[du, :, r0 : r0 + n, :] = v
                for dv in range(4):
                    if du + dv:
                        pv = lax.rem(at[OTHERS[c][1]] + dv, 4)
                        plane_copy(
                            c, du, dv, sum1.at[du, pv, pl.ds(r0, n)], got2.at[4 * du + dv - 1, pl.ds(r0, n)],
                            ks.at[c], kr.at[c])
            yield
        pieces = []
        for c in range(3):
            r0, n = SUM_ROWS[c]
            drain(ls.at[c], got1.at[:, :, :, pl.ds(r0, n)])
            drain(ks.at[c], got2.at[:, pl.ds(r0, n)])
            drain(kr.at[c], got2.at[:, pl.ds(r0, n)])
            v = sum1[0, at[OTHERS[c][1]], r0 : r0 + n, :]
            for i in range(15):
                v = v + got2[i, r0 : r0 + n, :]
            pieces.append(v)
        v = jnp.concatenate(pieces, axis=0)
        v = jnp.concatenate([v[:32], v[32:]], axis=1)
        result.append(jnp.where(live, v * (1.0 / (64 * 1024)), 0.0))

    def square(phase):
        high, low = halves(gath.at[phase])
        first, last = symmetric(high, low)
        cross = first[:, 256:512]
        return first[:, 0:256] + (cross + cross.T) + last

    def run(gen):
        for _ in gen:
            pass

    g = gather(0)
    next(g)
    load.wait()

    @pl.loop(0, 8)
    def _(m):
        cols = pl.ds(pl.multiple_of(m * 256, 256), 256)
        xt[cols, :] = x[:, cols].T

    run(g)
    project(0)
    out = []
    run(scatter(0, out))
    put_own(gath.at[1], out[0])
    run(gather(1))
    project(1)
    out = []
    s = scatter(1, out)
    next(s)
    factor_start(aug, square(1))
    for first, count in ((0, 5), (5, 1), (6, 2), (8, 3), (11, 5)):
        factor_part(aug, first, count)
        next(s, None)
    image = exact(out[0], aug[:, 256:512], ((1,), (1,)))
    put_own(gath.at[0], image)
    run(gather(2))
    project(0)

    first, last = symmetric(y[:, 0:256], y[:, 256:512])
    cross = first[:, 256:512]
    total = (first[:, 0:256] + (cross + cross.T) + last) * (1.0 / (64 * 1024))
    for c, (r, q) in enumerate(((0, 0), (0, 128), (128, 128))):
        mine[c] = total[r : r + 128, q : q + 128].reshape(4, 32, 128)
    for c, o in enumerate(ORDERS):
        copies(lambda pos: mine.at[c, pos], lambda d: mgot1.at[c, d - 1], ms.at[c, 0], mr.at[c, 0], o[0])
    factor_start(aug, square(0))
    factor_part(aug, 0, 3)
    for stage, had, now, pairs in ((1, None, mgot2, (3, 5)), (2, mgot2, mgot3, (8, 5)), (3, mgot3, mall, (13, 3))):
        for c, o in enumerate(ORDERS):
            drain(mr.at[c, stage - 1], mgot1.at[c])
            drain(ms.at[c, stage - 1], mgot1.at[c])
            if stage == 1:
                v = mine[c, at[o[0]]] + mgot1[c, 0] + mgot1[c, 1] + mgot1[c, 2]
            else:
                v = had[c, 0] + had[c, 1] + had[c, 2] + had[c, 3]
            axis = o[stage] if stage < 3 else o[0]
            now[c, at[axis]] = v
            view = now.at[c, at[axis]]
            copies(lambda pos: view, lambda d: view, ms.at[c, stage], mr.at[c, stage], axis)
        factor_part(aug, *pairs)
    low = aug[:, 256:512]
    for c in range(3):
        drain(mr.at[c, 3], mgot1.at[c])
        drain(ms.at[c, 3], mgot1.at[c])
    b00, b01, b11 = (mall[c].reshape(128, 128) for c in range(3))
    full = jnp.concatenate([jnp.concatenate([b00, b01], axis=1), jnp.concatenate([b01.T, b11], axis=1)], axis=0)
    left = exact(low, full, ((1,), (0,)))
    tbuf[0] = jnp.broadcast_to(jnp.sum(left * low, axis=(0, 1), keepdims=True), (8, 128))
    c = pltpu.make_async_remote_copy(
        src_ref=tbuf.at[0], dst_ref=tbuf.at[1], send_sem=ts, recv_sem=tr, device_id=(1 - blk, smp), device_id_type=MESH
    )
    c.start()
    ray = exact(left, low, ((1,), (1,)))
    basis[0] = exact(image, low, ((1,), (1,))) * math.sqrt(CAP)
    c.wait()
    both = tbuf[0, 0:1, 0:1] + tbuf[1, 0:1, 0:1]
    scaled[0] = ray * (2.0 * K) / both


def hand_out(basis, scaled, basis_out, scaled_out):
    basis_out[...] = basis[...]
    scaled_out[...] = scaled[...]


def body(genotypes, sizes, start):
    vm = pltpu.VMEM
    dma = pltpu.SemaphoreType.DMA
    shapes = (jax.ShapeDtypeStruct((1, 32, K), F32), jax.ShapeDtypeStruct((1, K, K), F32))
    results = pl.pallas_call(
        kernel,
        out_shape=shapes,
        in_specs=[
            pl.BlockSpec(memory_space=pl.ANY),
            pl.BlockSpec(memory_space=pl.ANY),
            pl.BlockSpec(memory_space=pl.ANY),
        ],
        out_specs=(pl.BlockSpec(memory_space=pltpu.VMEM), pl.BlockSpec(memory_space=pltpu.VMEM)),
        scratch_shapes=[
            vm((1024, CAP), BF16),
            vm((CAP, 1024), BF16),
            vm((2, 4, 4, 4, 128, 128), BF16),
            vm((1024, 512), BF16),
            vm((4, 4, 4, 64, 128), F32),
            vm((4, 4, 64, 128), F32),
            vm((3, 4, 4, 64, 128), F32),
            vm((15, 64, 128), F32),
            vm((K, 2 * K), F32),
            vm((3, 4, 32, 128), F32),
            vm((3, 3, 32, 128), F32),
            vm((3, 4, 32, 128), F32),
            vm((3, 4, 32, 128), F32),
            vm((3, 4, 32, 128), F32),
            vm((2, 8, 128), F32),
            pltpu.SMEM((1,), jnp.int32),
            vm((1, 32, K), F32),
            dma,
            dma((2,)),
            dma((3, 2)),
            dma((3, 4)),
            dma((3,)),
            dma((3,)),
            dma((3,)),
            dma((3, 4)),
            dma((3,)),
            dma((3,)),
            dma((3, 4)),
            dma((3, 4)),
            dma,
            dma,
        ],
        compiler_params=pltpu.CompilerParams(
            collective_id=0, has_side_effects=True, vmem_limit_bytes=60 * 2**20
        ),
    )(sizes, start, genotypes.reshape(genotypes.shape[1:]))
    return pl.pallas_call(hand_out, out_shape=shapes)(*results)


def solution(mesh):
    return jax.shard_map(
        body,
        mesh=mesh,
        in_specs=(P("blk", "smp", None), P("blk"), P("blk", "smp", None)),
        out_specs=(P("blk", "smp", None), P("blk", None, None)),
        check_vma=False,
    )
```
